128 devices in a mesh: tm: 16 (over y, x), space: 8 (over z, core).
Axes of the slice: x: 4, y: 4, z: 4, core: 2. Of those that a mesh axis runs over, the one named last changes fastest.
Arguments:
- queries: bfloat16 [32, 32, 16, 1024], P('tm', None, 'space'), may hold values from -16 to 16
- key_rows: bfloat16 [32, 32, 16, 1024], P('tm', None, 'space'), may hold values from -6 to 6
- value_rows: bfloat16 [32, 32, 16, 1024], P('tm', None, 'space'), may hold values from -5 to 5
- out_proj: bfloat16 [1024, 512], replicated, may hold values from -0.1875 to 0.1875
- conv_taps: bfloat16 [3, 3, 3, 512, 512], replicated, may hold values from -0.0546875 to 0.0546875
- cotangent: bfloat16 [32, 32, 16, 512], P('tm', None, 'space'), may hold values from -6 to 6
Outputs:
- conv_output: bfloat16 [32, 32, 16, 512], P('tm', None, 'space')
- grad_queries: bfloat16 [32, 32, 16, 1024], P('tm', None, 'space')
- grad_keys: bfloat16 [32, 32, 16, 1024], P('tm', None, 'space')
- grad_values: bfloat16 [32, 32, 16, 1024], P('tm', None, 'space')
The draws below stay inside these ranges and needn't reach their ends.
All inputs are finite; a program needn't handle non-finite values.
Results may differ from the reference program's by a relative error of at most 0.019.
Values may be sent and summed in bfloat16 or wider, within the bound.
No kernel may reach another device: no remote copies, remote signals or barrier semaphores. Data moves between devices by JAX's collectives and lax.ppermute only.
A program may use at most 128 MiB of HBM per device.

```python
import jax
import jax.numpy as jnp
from jax import lax

HEADS = 16
HEAD = 64
CH = 512
ROWS = 32
FRAMES = 32
COLS = 16


def attention_pair(key):
    base = jax.random.fold_in(key, 31)
    first_key, second_key = jax.random.split(base, 2)
    count = FRAMES * ROWS * COLS
    width = HEADS * HEAD
    query_new = jnp.clip(jax.random.normal(first_key, (count, width), jnp.float32), -4.0, 4.0)
    key_new = jnp.clip(jax.random.normal(second_key, (count, width), jnp.float32), -4.0, 4.0)
    return (query_new.reshape(FRAMES, ROWS, COLS, width), key_new.reshape(FRAMES, ROWS, COLS, width))


def draw_queries(key, part):
    return attention_pair(key)[0].astype(jnp.bfloat16)


def draw_key_rows(key, part):
    return attention_pair(key)[1].astype(jnp.bfloat16)


def steps_of(stream_key, shape, cuts, smallest, high):
    loudness, own = 1.0, jax.random.fold_in(stream_key, 6)
    for dim, blocks in cuts:
        heights = jnp.exp(jax.random.uniform(jax.random.fold_in(own, dim), (blocks,), jnp.float32, smallest / len(cuts), high / len(cuts)))
        loudness = loudness * jnp.repeat(heights, shape[dim] // blocks).reshape([-1 if axis == dim else 1 for axis in range(len(shape))])
    return loudness


def noise(own_key, shape, deviation, limit, cuts=(), kind=jnp.bfloat16):
    result = deviation * jax.random.normal(own_key, shape, jnp.float32)
    if cuts:
        result = result * steps_of(own_key, shape, cuts, -0.22, 0.18)
    return jnp.clip(result, -limit, limit).astype(kind)


def setup_inputs(seed: int = 0) -> dict:
    seeds = jax.random.split(jax.random.key(seed), 7)
    queries = draw_queries(jax.random.fold_in(seeds[6], 71), 0)
    key_rows = draw_key_rows(jax.random.fold_in(seeds[6], 71), 0)
    value_rows = noise(seeds[2], (FRAMES, ROWS, COLS, HEADS * HEAD), 1.0, 5.0, ((0, 16), (2, 8)))
    out_proj = noise(seeds[3], (HEADS * HEAD, CH), (HEADS * HEAD) ** -0.5, 0.1875)
    conv_taps = noise(seeds[4], (3, 3, 3, CH, CH), (27 * CH) ** -0.5, 0.0546875)
    cotangent = noise(seeds[5], (FRAMES, ROWS, COLS, CH), 1.0, 6.0, ((0, 16), (2, 8)))
    return {"queries": queries, "key_rows": key_rows, "value_rows": value_rows, "out_proj": out_proj, "conv_taps": conv_taps, "cotangent": cotangent}


HIGHEST = lax.Precision.HIGHEST


def heads_first(array):
    return array.reshape(FRAMES * ROWS * COLS, HEADS, HEAD).transpose(1, 0, 2)


def tokens_last(array):
    return array.transpose(1, 0, 2).reshape(FRAMES, ROWS, COLS, HEADS * HEAD)


def frozen(array):
    return lax.optimization_barrier(array.astype(jnp.bfloat16)).astype(jnp.float32)


def head_forward(operands):
    query_head = operands[0].astype(jnp.float32)
    key_head = operands[1].astype(jnp.float32)
    value_head = operands[2].astype(jnp.float32)
    scale = HEAD ** -0.5
    frame_tok = ROWS * COLS
    outputs = []
    logsums = []
    for frame in range(FRAMES):
        start = frame * frame_tok
        finish = start + frame_tok
        scores = jnp.dot(query_head[start:finish], key_head[:finish].T, precision=HIGHEST) * scale
        largest = jnp.max(scores, axis=1, keepdims=True)
        weights = jnp.exp(scores - largest)
        total = jnp.sum(weights, axis=1, keepdims=True)
        mixed = jnp.dot(frozen(weights), value_head[:finish], precision=HIGHEST) / total
        outputs.append(mixed.astype(jnp.bfloat16))
        logsums.append(largest[:, 0] + jnp.log(total[:, 0]))
    return jnp.concatenate(outputs, axis=0), jnp.concatenate(logsums, axis=0)


def head_backward(operands):
    query_head = operands[0].astype(jnp.float32)
    key_head = operands[1].astype(jnp.float32)
    value_head = operands[2].astype(jnp.float32)
    grad_head = operands[3].astype(jnp.float32)
    logsum = operands[4]
    delta = operands[5]
    scale = HEAD ** -0.5
    frame_tok = ROWS * COLS
    count = FRAMES * frame_tok
    query_parts = []
    grad_keys = jnp.zeros((count, HEAD), jnp.float32)
    grad_values = jnp.zeros((count, HEAD), jnp.float32)
    for frame in range(FRAMES):
        start = frame * frame_tok
        finish = start + frame_tok
        scores = jnp.dot(query_head[start:finish], key_head[:finish].T, precision=HIGHEST) * scale
        probs = jnp.exp(scores - logsum[start:finish, None])
        grad_values = grad_values.at[:finish].add(jnp.dot(frozen(probs).T, grad_head[start:finish], precision=HIGHEST))
        grad_probs = jnp.dot(grad_head[start:finish], value_head[:finish].T, precision=HIGHEST)
        grad_scores = frozen(probs * (grad_probs - delta[start:finish, None]))
        query_parts.append(jnp.dot(grad_scores, key_head[:finish], precision=HIGHEST) * scale)
        grad_keys = grad_keys.at[:finish].add(jnp.dot(grad_scores.T, query_head[start:finish], precision=HIGHEST) * scale)
    return jnp.concatenate(query_parts, axis=0), grad_keys, grad_values


def wrap_columns(padded):
    return jnp.concatenate([padded[:, :, -1:], padded, padded[:, :, :1]], axis=2)


def causal_conv(field, taps):
    padded = wrap_columns(jnp.pad(field, ((2, 0), (1, 1), (0, 0), (0, 0))))
    total = jnp.zeros((FRAMES * ROWS * COLS, CH), jnp.float32)
    for lag in range(3):
        for row_step in range(3):
            for col_step in range(3):
                window = padded[lag:lag + FRAMES, row_step:row_step + ROWS, col_step:col_step + COLS].reshape(-1, CH)
                total = total + jnp.dot(window, taps[lag, row_step, col_step], precision=HIGHEST)
    return total


def causal_conv_adjoint(field, taps):
    padded = wrap_columns(jnp.pad(field, ((0, 2), (1, 1), (0, 0), (0, 0))))
    total = jnp.zeros((FRAMES * ROWS * COLS, CH), jnp.float32)
    for lag in range(3):
        for row_step in range(3):
            for col_step in range(3):
                window = padded[2 - lag:2 - lag + FRAMES, 2 - row_step:2 - row_step + ROWS, 2 - col_step:2 - col_step + COLS].reshape(-1, CH)
                total = total + jnp.dot(window, taps[lag, row_step, col_step].T, precision=HIGHEST)
    return total


def reference(queries, key_rows, value_rows, out_proj, conv_taps, cotangent):
    query_heads = heads_first(queries)
    key_heads = heads_first(key_rows)
    value_heads = heads_first(value_rows)
    attended, logsums = lax.map(head_forward, (query_heads, key_heads, value_heads))
    attended_tokens = tokens_last(attended)
    projected = jnp.dot(attended_tokens.reshape(-1, HEADS * HEAD), out_proj, preferred_element_type=jnp.float32).astype(jnp.bfloat16)
    taps_wide = conv_taps.astype(jnp.float32)
    projected_wide = projected.astype(jnp.float32)
    mixed = causal_conv(projected_wide.reshape(FRAMES, ROWS, COLS, CH), taps_wide)
    conv_output = (projected_wide + mixed).astype(jnp.bfloat16).reshape(FRAMES, ROWS, COLS, CH)
    cot_wide = cotangent.astype(jnp.float32)
    grad_projected = (cot_wide.reshape(-1, CH) + causal_conv_adjoint(cot_wide, taps_wide)).astype(jnp.bfloat16)
    grad_attended = jnp.dot(grad_projected, out_proj.T, preferred_element_type=jnp.float32).astype(jnp.bfloat16)
    grad_heads = heads_first(grad_attended.reshape(FRAMES, ROWS, COLS, HEADS * HEAD))
    deltas = jnp.sum(grad_heads.astype(jnp.float32) * attended.astype(jnp.float32), axis=2)
    grad_q, grad_k, grad_v = lax.map(head_backward, (query_heads, key_heads, value_heads, grad_heads, logsums, deltas))
    return (conv_output,
            tokens_last(grad_q.astype(jnp.bfloat16)),
            tokens_last(grad_k.astype(jnp.bfloat16)),
            tokens_last(grad_v.astype(jnp.bfloat16)))
```

```python
import functools

import jax
import jax.numpy as jnp
from jax import lax
from jax.experimental import pallas as pl
from jax.experimental.pallas import tpu as pltpu
from jax.sharding import Mesh, PartitionSpec as P

HEAD = 64
NEGATIVE = -1e30
BF = jnp.bfloat16
F32 = jnp.float32
NN = (((1,), (0,)), ((), ()))
NT = (((1,), (1,)), ((), ()))
AXES = ("y", "x", "z", "c")
ROWS = 32
TOK = 512
SPAN = 4 * TOK
LIMIT = 60 * 2**20


def dot(a, b, dims=NN):
    return lax.dot_general(a, b, dims, preferred_element_type=F32)


def kernel_call(body, outs, scratch, args, grid=(1,), specs=None, us=1.0, name=None):
    def whole(shape):
        rank = len(shape)
        return pl.BlockSpec(shape, lambda *_: (0,) * rank)

    in_specs = [whole(a.shape) for a in args[1:]]
    for index, spec in (specs or {}).items():
        in_specs[index] = spec
    return pl.pallas_call(
        body,
        out_shape=outs,
        grid_spec=pltpu.PrefetchScalarGridSpec(
            num_scalar_prefetch=1,
            grid=grid,
            in_specs=in_specs,
            out_specs=[whole(o.shape) for o in outs],
            scratch_shapes=scratch,
        ),
        compiler_params=pltpu.CompilerParams(vmem_limit_bytes=LIMIT),
        cost_estimate=pl.CostEstimate(
            flops=int(us * 8e8), bytes_accessed=int(us * 1e6), transcendentals=0
        ),
        name=name,
    )(*args)


def struct(shape, dtype=BF):
    return jax.ShapeDtypeStruct(shape, dtype)


def write_pairs(low, high, out_ref):
    lane = lax.broadcasted_iota(jnp.int32, (1, 128), 1)
    for tile in range(8):
        a = low(tile)
        b = high(tile)
        even = jnp.where(lane < HEAD, a, pltpu.roll(b, HEAD, 1)).astype(BF)
        odd = jnp.where(lane < HEAD, pltpu.roll(a, HEAD, 1), b).astype(BF)
        for half, value in ((0, even), (1, odd)):
            for frame in range(2):
                for col in range(2):
                    row = (col * 2 + frame) * ROWS
                    out_ref[(2 * tile + half) * 2 + frame, col * ROWS : (col + 1) * ROWS, :] = value[
                        row : row + ROWS
                    ]


def read_pairs(in_ref, low, high):
    lane = lax.broadcasted_iota(jnp.int32, (1, 128), 1)
    for tile in range(8):
        for frame in range(2):
            even = in_ref[4 * tile + frame].astype(F32)
            odd = in_ref[4 * tile + 2 + frame].astype(F32)
            pair = []
            if low is not None:
                pair.append((low, jnp.where(lane < HEAD, even, pltpu.roll(odd, HEAD, 1))))
            if high is not None:
                pair.append((high, jnp.where(lane < HEAD, pltpu.roll(even, HEAD, 1), odd)))
            for target, value in pair:
                value = value.astype(BF)
                for col in range(2):
                    row = (col * 2 + frame) * ROWS
                    target[row : row + ROWS, tile * 128 : (tile + 1) * 128] = value[
                        col * ROWS : (col + 1) * ROWS
                    ]


def pack_body(pos_ref, a_ref, b_ref, out_ref):
    def tile_of(ref):
        return lambda tile: ref[:, tile * 128 : (tile + 1) * 128].astype(F32)

    write_pairs(tile_of(a_ref), tile_of(b_ref), out_ref)


def extend(own_ref, near_ref, sides, ext_ref, reverse):
    row = lax.broadcasted_iota(jnp.int32, (2 * ROWS, 1), 0) % ROWS
    own_left, own_right, near_left, near_right = sides
    for part, (mid, left, right) in enumerate(
        ((own_ref, own_left, own_right), (near_ref, near_left, near_right))
    ):
        first = 2 * part if reverse else 2 - 2 * part
        for col in range(4):
            ref = left if col == 0 else right if col == 3 else mid.at[col - 1]
            value = ref[...].astype(F32).reshape(2 * ROWS, -1)
            up = jnp.where(row == 0, 0.0, pltpu.roll(value, 1, 0))
            down = jnp.where(row == ROWS - 1, 0.0, pltpu.roll(value, 2 * ROWS - 1, 0))
            for shift, moved in enumerate((up, value, down)):
                ext_ref[shift, col, first : first + 2] = moved.astype(BF).reshape(2, ROWS, -1)


def conv_step(own_ref, near_ref, sides, taps_ref, ext_ref, acc_ref, reverse):
    step = pl.program_id(0)
    lag = step // 3
    shift = step % 3

    @pl.when(step == 0)
    def _():
        extend(own_ref, near_ref, sides, ext_ref, reverse)
        acc_ref[...] = own_ref[...].astype(F32).reshape(4 * ROWS, -1)

    if reverse:
        lag = 2 - lag
        shift = 2 - shift
    total = None
    for b in range(3):
        col = 2 - b if reverse else b
        window = ext_ref[shift, col : col + 2, pl.ds(lag, 2)].reshape(4 * ROWS, -1)
        part = dot(window, taps_ref[0, 0, b], NT if reverse else NN)
        total = part if total is None else total + part
    acc_ref[...] += total


def conv_body(pos_ref, own_ref, near_ref, ol, orr, nl, nr, taps_ref, out_ref, ext_ref, acc_ref):
    conv_step(own_ref, near_ref, (ol, orr, nl, nr), taps_ref, ext_ref, acc_ref, False)

    @pl.when(pl.program_id(0) == 8)
    def _():
        out_ref[...] = acc_ref[...].astype(BF)


def adjoint_body(
    pos_ref, own_ref, near_ref, ol, orr, nl, nr, taps_ref, proj_ref, q_ref, out_ref, ext_ref, acc_ref
):
    conv_step(own_ref, near_ref, (ol, orr, nl, nr), taps_ref, ext_ref, acc_ref, True)

    @pl.when(pl.program_id(0) == 8)
    def _():
        grad = acc_ref[...].astype(BF)

        def low(tile):
            return q_ref[:, tile * 128 : (tile + 1) * 128].astype(F32)

        def high(tile):
            return dot(grad, proj_ref[tile * 128 : (tile + 1) * 128, :], NT).astype(BF).astype(F32)

        write_pairs(low, high, out_ref)


def project_body(pos_ref, in_ref, proj_ref, out_ref, att_ref):
    read_pairs(in_ref, None, att_ref)
    out_ref[...] = dot(att_ref[...], proj_ref[...]).astype(BF)


def unpack_body(pos_ref, q_ref, kv_ref, gq_ref, gk_ref, gv_ref):
    read_pairs(q_ref, gq_ref, None)
    read_pairs(kv_ref, gk_ref, gv_ref)


def slot_frame(y, c, slot):
    own = 8 * y + c + 2 * slot
    mirrored = 8 * (3 - y) + (1 - c) + 2 * slot
    return jnp.where(slot < 2, own, mirrored)


def visible(frame, y, c):
    return jnp.clip(lax.shift_right_arithmetic(frame - 8 * y - c, 1) + 1, 0, 4)


def forward_body(pos_ref, qdo_ref, *refs):
    kv_refs = refs[:8]
    att_ref, stat_ref, kv_ref, ones_ref, max_ref, acc_ref = refs[8:]
    y = pos_ref[0]
    c = pos_ref[1]
    lane = lax.broadcasted_iota(jnp.int32, (1, 128), 1)
    one = jnp.ones((), BF)
    zero = jnp.zeros((), BF)
    for index in range(8):
        for block in range(4):
            rows = slice(block * TOK, (block + 1) * TOK)
            value = kv_refs[index][rows, :]
            kv_ref[index, rows, :] = value
            ones_ref[index, rows, :] = jnp.where(lane < HEAD, one, value)

    def per_slot(slot, _):
        frame = slot_frame(y, c, slot)
        rows = pl.ds(pl.multiple_of(slot * TOK, TOK), TOK)
        both = qdo_ref[rows, :]
        query = jnp.where(lane < HEAD, both, zero) * jnp.asarray(HEAD**-0.5, BF)
        max_ref[...] = jnp.full(max_ref.shape, NEGATIVE, F32)
        acc_ref[...] = jnp.zeros(acc_ref.shape, F32)

        def block(keys, values):
            scores = dot(query, keys, NT)
            before = max_ref[...]
            after = jnp.maximum(before, jnp.max(scores, axis=1, keepdims=True))
            weights = jnp.exp(scores - after).astype(BF)
            acc_ref[...] = acc_ref[...] * jnp.exp(before - after) + dot(weights, values)
            max_ref[...] = after

        def per_array(index, _):
            delta = jnp.where(index < 4, index // 2, jnp.where(index < 6, 3, 2))
            y_keys = lax.rem(y - delta + 4, 4)
            c_keys = lax.rem(c + index, 2)
            count = visible(frame, y_keys, c_keys)

            @pl.when(count == 4)
            def _():
                block(kv_ref[index], ones_ref[index])

            @pl.when(count < 4)
            def _():
                def per_block(j, _):
                    part = pl.ds(pl.multiple_of(j * TOK, TOK), TOK)
                    block(kv_ref[index, part, :], ones_ref[index, part, :])
                    return 0

                lax.fori_loop(0, count, per_block, 0)

            return 0

        lax.fori_loop(0, 8, per_array, 0)
        acc = acc_ref[...]
        total = acc[:, 0:1]
        att = jnp.where(lane < HEAD, 0.0, acc / total).astype(BF)
        att_ref[rows, :] = att
        delta = jnp.sum(att.astype(F32) * both.astype(F32), axis=1, keepdims=True)
        logsum = max_ref[...] + jnp.log(total)
        stats = jnp.where(lane == 0, logsum, delta)
        stat_ref[:, rows] = stats.T[0:8, :]
        return 0

    lax.fori_loop(0, 4, per_slot, 0)


def backward_body(step, last, pos_ref, qdo_ref, stat_ref, same_ref, other_ref, *refs):
    if step is None:
        raise ValueError
    refs = list(refs)
    seed_ref = refs.pop(0) if not refs[0].shape == same_ref.shape else None
    same_out, other_out, dq_out, turned_ref, acc_ref, query_ref, dq_ref = refs
    y = pos_ref[0]
    c = pos_ref[1]
    y_keys = lax.rem(y + step, 4)
    lane = lax.broadcasted_iota(jnp.int32, (1, 128), 1)
    zero = jnp.zeros((), BF)
    eye = (
        lax.broadcasted_iota(jnp.int32, (128, 128), 0)
        == lax.broadcasted_iota(jnp.int32, (128, 128), 1)
    ).astype(BF)
    arrays = (same_ref, other_ref)
    for index in range(2):
        for block in range(4):
            rows = slice(block * TOK, (block + 1) * TOK)
            turned_ref[index, :, rows] = dot(eye, arrays[index][rows, :], NT).astype(BF)
            acc_ref[index, rows, :] = jnp.zeros((TOK, 128), F32)

    def per_slot(slot, _):
        frame = slot_frame(y, c, slot)
        rows = pl.ds(pl.multiple_of(slot * TOK, TOK), TOK)
        both = qdo_ref[rows, :]
        query_ref[0:TOK, :] = jnp.where(lane < HEAD, both, zero) * jnp.asarray(HEAD**-0.5, BF)
        query_ref[TOK : 2 * TOK, :] = jnp.where(lane < HEAD, zero, both)
        stats = stat_ref[:, rows]
        logsum = stats[0:1, :]
        delta = stats[1:2, :]
        if seed_ref is None:
            dq_ref[...] = jnp.zeros(dq_ref.shape, F32)
        else:
            dq_ref[...] = seed_ref[:, rows]

        def pairs(index, part):
            keys = arrays[index][part, :]
            query = query_ref[0:TOK, :]
            grad = query_ref[TOK : 2 * TOK, :]
            probs = jnp.exp(dot(keys, query, NT) - logsum)
            inner = (probs * (dot(keys, grad, NT) - delta)).astype(BF)
            acc_ref[index, part, :] += dot(inner, query) + dot(probs.astype(BF), grad)
            dq_ref[...] += dot(turned_ref[index, :, part], inner)

        for index in range(2):
            count = visible(frame, y_keys, c if index == 0 else 1 - c)

            def double(j, _, index=index):
                pairs(index, pl.ds(pl.multiple_of(j * 2 * TOK, 2 * TOK), 2 * TOK))
                return 0

            lax.fori_loop(0, count // 2, double, 0)

            @pl.when(lax.rem(count, 2) == 1)
            def _(index=index, count=count):
                pairs(index, pl.ds(pl.multiple_of((count - 1) * TOK, TOK), TOK))

        if last:
            scaled = dq_ref[...] * HEAD**-0.5
            dq_out[rows, :] = scaled.T.astype(BF)
        else:
            dq_out[:, rows] = dq_ref[...]
        return 0

    lax.fori_loop(0, 4, per_slot, 0)
    same_out[...] = acc_ref[0].astype(BF)
    other_out[...] = acc_ref[1].astype(BF)


def shift_y(value, steps):
    return lax.ppermute(value, "y", [(i, (i + steps) % 4) for i in range(4)])


def swap_core(value):
    return lax.ppermute(value, "c", [(0, 1), (1, 0)])


def mirror(value):
    return lax.ppermute(
        value, ("y", "c"), [(y * 2 + c, (3 - y) * 2 + 1 - c) for y in range(4) for c in range(2)]
    )


def halo(own, forward):
    step = 1 if forward else -1

    def route(frames, cols):
        return [
            (t * 8 + s, (t + frames) * 8 + (s + cols) % 8)
            for t in range(16)
            for s in range(8)
            if 0 <= t + frames < 16
        ]

    near = lax.ppermute(own, AXES, route(step, 0))
    own_left = lax.ppermute(own[1], AXES, route(0, 1))
    own_right = lax.ppermute(own[0], AXES, route(0, -1))
    near_left = lax.ppermute(own[1], AXES, route(step, 1))
    near_right = lax.ppermute(own[0], AXES, route(step, -1))
    return near, own_left, own_right, near_left, near_right


def exchange(value):
    return lax.all_to_all(value, ("x", "z", "c"), split_axis=0, concat_axis=0, tiled=True)


def columns_first(array):
    return array.transpose(2, 0, 1, 3)


def flat(array):
    return columns_first(array).reshape(4 * ROWS, -1)


def tokens_back(array):
    return array.reshape(2, 2, ROWS, -1).transpose(1, 2, 0, 3)


def shards(queries, key_rows, value_rows, out_proj, conv_taps, cotangent):
    channels = out_proj.shape[1]
    pos = jnp.stack([lax.axis_index("y"), lax.axis_index("c")]).astype(jnp.int32)
    packed = struct((32, 64, 128))
    taps_spec = pl.BlockSpec((1, 1, 3, channels, channels), lambda t, *_: (t // 3, t % 3, 0, 0, 0))
    conv_scratch = [
        pltpu.VMEM((3, 4, 4, ROWS, channels), BF),
        pltpu.VMEM((4 * ROWS, channels), F32),
    ]

    (pairs,) = kernel_call(
        pack_body, [packed], [], (pos, flat(key_rows), flat(value_rows)), us=2.0, name="pack"
    )
    kv_own = exchange(pairs).reshape(SPAN, 128)

    cot = columns_first(cotangent)
    (qdo,) = kernel_call(
        adjoint_body,
        [packed],
        conv_scratch,
        (pos, cot, *halo(cot, False), conv_taps, out_proj, flat(queries)),
        grid=(9,),
        specs={6: taps_spec},
        us=10.0,
        name="adjoint",
    )
    kv_same = {0: kv_own}
    for steps in (1, 3, 2):
        kv_same[steps] = shift_y(kv_own, steps)
    kv_other = {steps: swap_core(kv_same[steps]) for steps in (0, 1, 3, 2)}

    qdo = exchange(qdo).reshape(SPAN, 128)
    qdo = jnp.concatenate([qdo[: SPAN // 2], mirror(qdo[SPAN // 2 :])], axis=0)

    arrays = []
    for steps in (0, 1, 3, 2):
        arrays += [kv_same[steps], kv_other[steps]]
    att, stats = kernel_call(
        forward_body,
        [struct((SPAN, 128)), struct((8, SPAN), F32)],
        [
            pltpu.VMEM((8, SPAN, 128), BF),
            pltpu.VMEM((8, SPAN, 128), BF),
            pltpu.VMEM((TOK, 1), F32),
            pltpu.VMEM((TOK, 128), F32),
        ],
        (pos, qdo, *arrays),
        us=35.0,
        name="forward",
    )

    seed = None
    received = []
    for steps in (2, 1, 3, 0):
        last = steps == 0
        behind = (4 - steps) % 4
        extra = () if seed is None else (seed,)
        same, other, seed = kernel_call(
            functools.partial(backward_body, steps, last),
            [
                struct((SPAN, 128)),
                struct((SPAN, 128)),
                struct((SPAN, 128)) if last else struct((128, SPAN), F32),
            ],
            [
                pltpu.VMEM((2, 128, SPAN), BF),
                pltpu.VMEM((2, SPAN, 128), F32),
                pltpu.VMEM((2 * TOK, 128), BF),
                pltpu.VMEM((128, TOK), F32),
            ],
            (pos, qdo, stats, kv_same[behind], kv_other[behind], *extra),
            us=15.0,
            name=f"backward{steps}",
        )
        joined = same.astype(F32) + swap_core(other).astype(F32)
        received.append(joined if last else shift_y(joined.astype(BF), steps).astype(F32))
    grad_kv = (received[0] + received[1] + received[2] + received[3]).astype(BF)

    att = jnp.concatenate([att[: SPAN // 2], mirror(att[SPAN // 2 :])], axis=0)
    att = exchange(att.reshape(32, 64, 128))
    (projected,) = kernel_call(
        project_body,
        [struct((4 * ROWS, channels))],
        [pltpu.VMEM((4 * ROWS, 1024), BF)],
        (pos, att, out_proj),
        us=2.0,
        name="project",
    )
    projected = projected.reshape(2, 2, ROWS, channels)
    (conv,) = kernel_call(
        conv_body,
        [struct((4 * ROWS, channels))],
        conv_scratch,
        (pos, projected, *halo(projected, True), conv_taps),
        grid=(9,),
        specs={6: taps_spec},
        us=8.0,
        name="conv",
    )

    grad_q = jnp.concatenate([seed[: SPAN // 2], mirror(seed[SPAN // 2 :])], axis=0)
    grad_q = exchange(grad_q.reshape(32, 64, 128))
    grad_kv = exchange(grad_kv.reshape(32, 64, 128))
    grads = kernel_call(
        unpack_body,
        [struct((4 * ROWS, 1024))] * 3,
        [],
        (pos, grad_q, grad_kv),
        us=2.0,
        name="unpack",
    )
    return (tokens_back(conv), *(tokens_back(g) for g in grads))


def solution(mesh):
    grid = Mesh(mesh.devices.reshape(4, 4, 4, 2), AXES)
    spec = P(("y", "x"), None, ("z", "c"), None)
    return jax.shard_map(
        shards,
        mesh=grid,
        in_specs=(spec, spec, spec, P(), P(), spec),
        out_specs=(spec,) * 4,
        check_vma=False,
    )
```

```python
import functools

import jax
import jax.numpy as jnp
from jax import lax
from jax.experimental import pallas as pl
from jax.experimental.pallas import tpu as pltpu
from jax.sharding import Mesh, PartitionSpec as P


HEAD = 64
NEGATIVE = -1e30
BF = jnp.bfloat16
F32 = jnp.float32
NN = (((1,), (0,)), ((), ()))
NT = (((1,), (1,)), ((), ()))
AXES = ("y", "x", "z", "c")
ROWS = 32
TOK = 512
SPAN = 4 * TOK
LIMIT = 60 * 2**20


def dot(a, b, dims=NN):
    return lax.dot_general(a, b, dims, preferred_element_type=F32)


def kernel_call(body, outs, scratch, args, grid=(1,), specs=None, us=1.0):
    def whole(shape):
        rank = len(shape)
        return pl.BlockSpec(shape, lambda *_: (0,) * rank)

    in_specs = [whole(a.shape) for a in args]
    for index, spec in (specs or {}).items():
        in_specs[index] = spec
    return pl.pallas_call(
        body,
        out_shape=outs,
        grid=grid,
        in_specs=in_specs,
        out_specs=[whole(o.shape) for o in outs],
        scratch_shapes=scratch,
        compiler_params=pltpu.CompilerParams(vmem_limit_bytes=LIMIT),
        cost_estimate=pl.CostEstimate(
            flops=int(us * 8e8), bytes_accessed=int(us * 1e6), transcendentals=0
        ),
    )(*args)


def struct(shape, dtype=BF):
    return jax.ShapeDtypeStruct(shape, dtype)


def write_rows(value, head, place, out_ref, stage_ref):
    for frame in range(2):
        stage_ref[head, pl.ds(frame, ROWS, stride=2), :] = value[frame * ROWS : (frame + 1) * ROWS]
    out_ref[:, head, :, place] = stage_ref[head].reshape(4, 2, 8, 128).astype(BF)


def write_columns(tile_of, out_ref, stage_ref, place):
    lane = lax.broadcasted_iota(jnp.int32, (1, 128), 1)
    for tile in range(8):
        value = tile_of(tile)
        first = value[: 2 * ROWS]
        second = value[2 * ROWS :]
        even = jnp.where(lane < HEAD, first, pltpu.roll(second, HEAD, 1))
        odd = jnp.where(lane < HEAD, pltpu.roll(first, HEAD, 1), second)
        write_rows(even, 2 * tile, place, out_ref, stage_ref)
        write_rows(odd, 2 * tile + 1, place, out_ref, stage_ref)


def write_pairs(low, high, out_ref, stage_ref, place):
    lane = lax.broadcasted_iota(jnp.int32, (1, 128), 1)
    for tile in range(8):
        a = low(tile)
        b = high(tile)
        even = jnp.where(lane < HEAD, a, pltpu.roll(b, HEAD, 1))
        odd = jnp.where(lane < HEAD, pltpu.roll(a, HEAD, 1), b)
        for half, value in ((0, even), (1, odd)):
            for col in range(2):
                part = value[col * 2 * ROWS : (col + 1) * 2 * ROWS]
                write_rows(part, 2 * tile + half, place + col, out_ref, stage_ref)


def read_rows(value, slot, col, tile, target, stage_ref):
    stage_ref[slot] = value
    for frame in range(2):
        row = (col * 2 + frame) * ROWS
        target[row : row + ROWS, tile * 128 : (tile + 1) * 128] = stage_ref[
            slot, pl.ds(frame, ROWS, stride=2), :
        ].astype(BF)


def heads_of(in_ref, tile, place):
    even = in_ref[:, 2 * tile, :, place].astype(F32).reshape(2 * ROWS, 128)
    odd = in_ref[:, 2 * tile + 1, :, place].astype(F32).reshape(2 * ROWS, 128)
    lane = lax.broadcasted_iota(jnp.int32, (1, 128), 1)
    low = jnp.where(lane < HEAD, even, pltpu.roll(odd, HEAD, 1))
    high = jnp.where(lane < HEAD, pltpu.roll(even, HEAD, 1), odd)
    return low, high


def read_columns(in_ref, target, stage_ref, place):
    for tile in range(8):
        low, high = heads_of(in_ref, tile, place)
        read_rows(low, 2 * tile, 0, tile, target, stage_ref)
        read_rows(high, 2 * tile + 1, 1, tile, target, stage_ref)


def read_pairs(in_ref, low_ref, high_ref, stage_ref, place):
    for tile in range(8):
        for col in range(2):
            low, high = heads_of(in_ref, tile, place + col)
            read_rows(low, 2 * tile, col, tile, low_ref, stage_ref)
            read_rows(high, 2 * tile + 1, col, tile, high_ref, stage_ref)


def tiles_of(ref):
    return lambda tile: ref[:, tile * 128 : (tile + 1) * 128].astype(F32)


def pack_body(q_ref, k_ref, v_ref, out_ref, stage_ref):
    write_columns(tiles_of(q_ref), out_ref, stage_ref, 0)
    write_pairs(tiles_of(k_ref), tiles_of(v_ref), out_ref, stage_ref, 1)


def extend(own_ref, near_ref, ext_ref, reverse):
    row = lax.broadcasted_iota(jnp.int32, (2 * ROWS, 1), 0) % ROWS
    for part, ref in enumerate((own_ref, near_ref)):
        first = 2 * part if reverse else 2 - 2 * part
        for col in range(4):
            value = ref[col].astype(F32).reshape(2 * ROWS, -1)
            up = jnp.where(row == 0, 0.0, pltpu.roll(value, 1, 0))
            down = jnp.where(row == ROWS - 1, 0.0, pltpu.roll(value, 2 * ROWS - 1, 0))
            for shift, moved in enumerate((up, value, down)):
                ext_ref[shift, col, first : first + 2] = moved.astype(BF).reshape(2, ROWS, -1)


def conv_step(own_ref, near_ref, taps_ref, ext_ref, acc_ref, reverse):
    step = pl.program_id(0)
    lag = step // 3
    shift = step % 3

    @pl.when(step == 0)
    def _():
        extend(own_ref, near_ref, ext_ref, reverse)
        acc_ref[...] = own_ref[1:3].astype(F32).reshape(4 * ROWS, -1)

    if reverse:
        lag = 2 - lag
        shift = 2 - shift
    total = None
    for b in range(3):
        col = 2 - b if reverse else b
        window = ext_ref[shift, col : col + 2, pl.ds(lag, 2)].reshape(4 * ROWS, -1)
        part = dot(window, taps_ref[0, 0, b], NT if reverse else NN)
        total = part if total is None else total + part
    acc_ref[...] += total


def conv_body(own_ref, near_ref, taps_ref, out_ref, ext_ref, acc_ref):
    conv_step(own_ref, near_ref, taps_ref, ext_ref, acc_ref, False)

    @pl.when(pl.program_id(0) == 8)
    def _():
        out_ref[...] = acc_ref[...].astype(BF)


def adjoint_body(own_ref, near_ref, taps_ref, proj_ref, out_ref, ext_ref, acc_ref, stage_ref):
    conv_step(own_ref, near_ref, taps_ref, ext_ref, acc_ref, True)

    @pl.when(pl.program_id(0) == 8)
    def _():
        grad = acc_ref[...].astype(BF)

        def tile_of(tile):
            return dot(grad, proj_ref[tile * 128 : (tile + 1) * 128, :], NT)

        write_columns(tile_of, out_ref, stage_ref, 0)


def project_body(in_ref, proj_ref, out_ref, att_ref, stage_ref):
    read_columns(in_ref, att_ref, stage_ref, 0)
    out_ref[...] = dot(att_ref[...], proj_ref[...]).astype(BF)


def unpack_body(in_ref, gq_ref, gk_ref, gv_ref, stage_ref):
    read_columns(in_ref, gq_ref, stage_ref, 0)
    read_pairs(in_ref, gk_ref, gv_ref, stage_ref, 1)


def join_columns(value, out_ref, base, roll_low):
    lane = lax.broadcasted_iota(jnp.int32, (1, 128), 1)
    for x in range(4):
        first = value[x * 128 : x * 128 + 64]
        second = value[x * 128 + 64 : (x + 1) * 128]
        if roll_low:
            first = pltpu.roll(first, HEAD, 1)
        else:
            second = pltpu.roll(second, HEAD, 1)
        out_ref[pl.ds(pl.multiple_of(base + x * 64, 64), 64), :] = jnp.where(
            lane < HEAD, first, second
        ).astype(BF)


def split_columns(value, out_ref, group, high):
    lane = lax.broadcasted_iota(jnp.int32, (1, 128), 1)
    keep = lane >= HEAD if high else lane < HEAD
    moved = pltpu.roll(value, HEAD, 1)
    first, second = (moved, value) if high else (value, moved)
    out_ref[group * 128 : group * 128 + 64, :] = jnp.where(keep, first, 0.0).astype(BF)
    out_ref[group * 128 + 64 : (group + 1) * 128, :] = jnp.where(keep, second, 0.0).astype(BF)


def forward_body(number, first, last, *refs):
    refs = list(refs)
    kv_refs = [refs.pop(0) for _ in range(number)]
    source_ref = refs.pop(0)
    if not first:
        seed_ref = refs.pop(0)
    if last:
        do_ref = refs.pop(0)
        att_ref, stat_ref, grad_ref, kv_ref, max_ref, acc_ref, sems = refs
        query_ref = source_ref
    elif first:
        query_ref, state_ref, kv_ref, max_ref, acc_ref, sems = refs
    else:
        state_ref, kv_ref, max_ref, acc_ref, sems = refs
        query_ref = source_ref
    lane = lax.broadcasted_iota(jnp.int32, (1, 128), 1)
    one = jnp.ones((), BF)
    copies = [
        pltpu.make_async_copy(kv_refs[i], kv_ref.at[:, :, i], sems.at[i]) for i in range(number)
    ]
    for copy in copies:
        copy.start()
    for group in range(16):
        rows = slice(group * 8, (group + 1) * 8)
        if first:
            value = source_ref[rows].astype(F32).reshape(64, 128) * HEAD**-0.5
            split_columns(value, query_ref, group, False)
        if last:
            split_columns(do_ref[rows].astype(F32).reshape(64, 128), grad_ref, group, True)
    for copy in copies:
        copy.wait()

    def per_block(block, _):
        start = block * TOK
        rows = pl.ds(pl.multiple_of(start, TOK), TOK)
        if first:
            max_ref[...] = jnp.full(max_ref.shape, NEGATIVE, F32)
            acc_ref[...] = jnp.zeros(acc_ref.shape, F32)
        else:
            max_ref[...] = jnp.broadcast_to(seed_ref[rows, 1:2], max_ref.shape)
            acc_ref[...] = seed_ref[rows, :]

        def update(part, scores, keys):
            before = max_ref[part, :]
            high = jnp.max(scores, axis=1, keepdims=True)
            after = jnp.maximum(before, jnp.broadcast_to(high, before.shape))
            shift = jnp.concatenate([after] * (scores.shape[1] // 128), axis=1)
            weights = jnp.exp(scores - shift).astype(BF)
            moved = dot(weights, jnp.where(lane < HEAD, one, keys))
            acc_ref[part, :] = acc_ref[part, :] * jnp.exp(before - after) + moved
            max_ref[part, :] = after

        def whole(index, _):
            keys = kv_ref[index].reshape(number * TOK, 128)
            update(slice(None), dot(query_ref[rows, :], keys, NT), keys)
            return 0

        lax.fori_loop(0, block, whole, 0)
        for half in range(2):
            count = TOK - 256 * half
            query = query_ref[pl.ds(pl.multiple_of(start + half * 256, 256), count), :]
            keys = kv_ref[block, 2 * half : 2 * half + 2].reshape(number * 256, 128)
            row = lax.broadcasted_iota(jnp.int32, (count, 1), 0)
            key = lax.broadcasted_iota(jnp.int32, (1, number * 256), 1)
            hidden = row // 128 * 2 + row % 2 < key // (number * 128) * 2 + key % 2
            scores = jnp.where(hidden, NEGATIVE, dot(query, keys, NT))
            update(slice(half * 256, TOK), scores, keys)
        acc = acc_ref[...]
        if not last:
            state_ref[rows, :] = jnp.where(lane == 1, max_ref[...], acc)
            return 0
        total = acc[:, 0:1]
        att = (acc / total).astype(BF).astype(F32)
        delta = jnp.sum(att * grad_ref[rows, :].astype(F32), axis=1, keepdims=True)
        logsum = max_ref[:, 0:1] + jnp.log(total)
        stat_ref[:, rows] = jnp.where(lane == 0, logsum, delta).T[0:8, :]
        join_columns(att, att_ref, block * 256, True)
        return 0

    lax.fori_loop(0, 4, per_block, 0)


def backward_body(first, last, same_ref, other_ref, query_ref, grad_ref, stat_ref, *refs):
    refs = list(refs)
    seed_ref = None if first else refs.pop(0)
    same_out, other_out, dq_out, kv_ref, turned_ref, acc_ref, dq_ref = refs
    eye = (
        lax.broadcasted_iota(jnp.int32, (128, 128), 0)
        == lax.broadcasted_iota(jnp.int32, (128, 128), 1)
    ).astype(BF)
    kv_ref[:, :, 0] = same_ref[...]
    kv_ref[:, :, 1] = other_ref[...]
    dq_ref[...] = jnp.zeros(dq_ref.shape, F32) if first else seed_ref[...]

    def per_keys(block, _):
        turned_ref[...] = dot(eye, kv_ref[block].reshape(2 * TOK, 128), NT).astype(BF)
        acc_ref[...] = jnp.zeros(acc_ref.shape, F32)

        def pairs(start, count, part, masked):
            rows = pl.ds(pl.multiple_of(start, 128), count)
            query = query_ref[rows, :]
            grad = grad_ref[rows, :]
            stats = stat_ref[:, rows]
            keys = kv_ref[block].reshape(2 * TOK, 128)[part]
            probs = jnp.exp(dot(keys, query, NT) - stats[0:1, :])
            if masked:
                key = lax.broadcasted_iota(jnp.int32, (keys.shape[0], 1), 0)
                row = lax.broadcasted_iota(jnp.int32, (1, count), 1)
                hidden = key // 256 * 2 + key % 2 > row // 128 * 2 + row % 2
                probs = jnp.where(hidden, 0.0, probs)
            inner = (probs * (dot(keys, grad, NT) - stats[1:2, :])).astype(BF)
            acc_ref[part, :] += dot(inner, query) + dot(probs.astype(BF), grad)
            dq_ref[:, rows] += dot(turned_ref[:, part], inner)

        def whole(later, _):
            pairs(later * TOK, TOK, slice(0, 2 * TOK), False)
            return 0

        lax.fori_loop(block + 1, 4, whole, 0)
        pairs(block * TOK, TOK, slice(0, TOK), True)
        pairs(block * TOK + 256, 256, slice(TOK, 2 * TOK), True)
        total = acc_ref[...].astype(BF).reshape(4, 2, 128, 128)
        same_out[block] = total[:, 0]
        other_out[block] = total[:, 1]
        return 0

    lax.fori_loop(0, 4, per_keys, 0)
    if last:
        for block in range(4):
            value = (dq_ref[:, block * TOK : (block + 1) * TOK] * HEAD**-0.5).T
            join_columns(value, dq_out, block * 256, False)
    else:
        dq_out[...] = dq_ref[...]


def shift_y(value, steps):
    return lax.ppermute(value, "y", [(i, (i + steps) % 4) for i in range(4)])


def swap_core(value):
    return lax.ppermute(value, "c", [(0, 1), (1, 0)])


def halo(own, forward):
    step = 1 if forward else -1

    def turn(value, cols):
        pairs = [(i, (i + cols) % 8) for i in range(8)]
        return lax.ppermute(value, ("z", "c"), pairs)

    left = turn(own[1:], 1)
    right = turn(own[:1], -1)
    wide = jnp.concatenate([left, own, right], axis=0)
    frames = [(t, t + step) for t in range(16) if 0 <= t + step < 16]
    return wide, lax.ppermute(wide, ("y", "x"), frames)


def exchange_all(value):
    split = value.reshape(128, -1, 128)
    return lax.all_to_all(split, AXES, split_axis=0, concat_axis=0, tiled=True)


def columns_first(array):
    return array.transpose(2, 0, 1, 3)


def flat(array):
    return columns_first(array).reshape(4 * ROWS, -1)


def tokens_back(array):
    return array.reshape(2, 2, ROWS, -1).transpose(1, 2, 0, 3)


def shards(queries, key_rows, value_rows, out_proj, conv_taps, cotangent):
    channels = out_proj.shape[1]
    stage = pltpu.VMEM((16, 2 * ROWS, 128), F32)
    taps_spec = pl.BlockSpec((1, 1, 3, channels, channels), lambda t: (t // 3, t % 3, 0, 0, 0))
    conv_scratch = [
        pltpu.VMEM((3, 4, 4, ROWS, channels), BF),
        pltpu.VMEM((4 * ROWS, channels), F32),
    ]
    grouped = (4, 4, 128, 128)

    near = halo(columns_first(cotangent), False)
    (packed,) = kernel_call(
        pack_body,
        [struct((4, 16, 2, 3, 8, 128))],
        [stage],
        (flat(queries), flat(key_rows), flat(value_rows)),
        us=4.0,
    )
    packed = exchange_all(packed)
    (grad,) = kernel_call(
        adjoint_body,
        [struct((4, 16, 2, 1, 8, 128))],
        [*conv_scratch, stage],
        (*near, conv_taps, out_proj),
        grid=(9,),
        specs={2: taps_spec},
        us=12.0,
    )
    packed, grad = lax.optimization_barrier((packed, grad))
    source = packed[:, :8]
    kv_same = {0: packed[:, 8:].reshape(grouped)}
    for steps in (1, 3, 2):
        kv_same[steps] = shift_y(kv_same[0], steps)
    kv_other = {steps: swap_core(kv_same[steps]) for steps in (0, 1, 3, 2)}
    grad = exchange_all(grad)

    def attend(arrays, extra, outs, us, first=False, last=False):
        number = len(arrays)
        return kernel_call(
            functools.partial(forward_body, number, first, last),
            outs,
            [
                pltpu.VMEM((4, 4, number, 128, 128), BF),
                pltpu.VMEM((TOK, 128), F32),
                pltpu.VMEM((TOK, 128), F32),
                pltpu.SemaphoreType.DMA((number,)),
            ],
            (*arrays, *extra),
            specs={index: pl.BlockSpec(memory_space=pl.ANY) for index in range(number)},
            us=us,
        )

    state = struct((SPAN, 128), F32)
    query, seed = attend(
        [kv_same[0], kv_other[0]], (source,), [struct((SPAN, 128)), state], 10.0, True
    )
    (seed,) = attend([kv_same[i] for i in (1, 3, 2)], (query, seed), [state], 15.0)
    att, stats, grad = attend(
        [kv_other[i] for i in (1, 3, 2)],
        (query, seed, grad),
        [struct((SPAN // 2, 128)), struct((8, SPAN), F32), struct((SPAN, 128))],
        15.0,
        last=True,
    )
    att = exchange_all(att).reshape(4, 16, 2, 1, 8, 128)

    seed = None
    total = None
    for steps in (2, 1, 3, 0):
        last = steps == 0
        same, other, seed = kernel_call(
            functools.partial(backward_body, seed is None, last),
            [
                struct(grouped),
                struct(grouped),
                struct((SPAN // 2, 128)) if last else struct((128, SPAN), F32),
            ],
            [
                pltpu.VMEM((4, 4, 2, 128, 128), BF),
                pltpu.VMEM((128, 2 * TOK), BF),
                pltpu.VMEM((2 * TOK, 128), F32),
                pltpu.VMEM((128, SPAN), F32),
            ],
            (kv_same[steps], kv_other[steps], query, grad, stats)
            + (() if seed is None else (seed,)),
            us=16.0,
        )
        joined = same.astype(F32) + swap_core(other).astype(F32)
        if not last:
            joined = shift_y(joined.astype(BF), 4 - steps).astype(F32)
        total = joined if total is None else total + joined
    (projected,) = kernel_call(
        project_body,
        [struct((4 * ROWS, channels))],
        [pltpu.VMEM((4 * ROWS, 1024), BF), stage],
        (att, out_proj),
        us=3.0,
    )
    near = halo(projected.reshape(2, 2, ROWS, channels), True)
    (conv,) = kernel_call(
        conv_body,
        [struct((4 * ROWS, channels))],
        conv_scratch,
        (*near, conv_taps),
        grid=(9,),
        specs={2: taps_spec},
        us=10.0,
    )
    grads = jnp.concatenate(
        [seed.reshape(128, 8, 128), total.astype(BF).reshape(128, 16, 128)], axis=1
    )
    grads = exchange_all(grads).reshape(4, 16, 2, 3, 8, 128)
    grads = kernel_call(unpack_body, [struct((4 * ROWS, 1024))] * 3, [stage], (grads,), us=4.0)
    return (tokens_back(conv), *(tokens_back(g) for g in grads))


def solution(mesh):
    grid = Mesh(mesh.devices.reshape(4, 4, 4, 2), AXES)
    spec = P(("y", "x"), None, ("z", "c"), None)
    return jax.shard_map(
        shards,
        mesh=grid,
        in_specs=(spec, spec, spec, P(), P(), spec),
        out_specs=(spec,) * 4,
        check_vma=False,
    )
```

```python
import functools

import jax
import jax.numpy as jnp
from jax import lax
from jax.experimental import pallas as pl
from jax.experimental.pallas import tpu as pltpu
from jax.sharding import Mesh, PartitionSpec as P


HEAD = 64
NEGATIVE = -1e30
BF = jnp.bfloat16
F32 = jnp.float32
NN = (((1,), (0,)), ((), ()))
NT = (((1,), (1,)), ((), ()))
AXES = ("y", "x", "z", "c")
ROWS = 32
TOK = 512
SPAN = 4 * TOK
LIMIT = 60 * 2**20


def dot(a, b, dims=NN):
    return lax.dot_general(a, b, dims, preferred_element_type=F32)


def kernel_call(body, outs, scratch, args, grid=(1,), specs=None, us=1.0):
    def whole(shape):
        rank = len(shape)
        return pl.BlockSpec(shape, lambda *_: (0,) * rank)

    in_specs = [whole(a.shape) for a in args]
    for index, spec in (specs or {}).items():
        in_specs[index] = spec
    return pl.pallas_call(
        body,
        out_shape=outs,
        grid=grid,
        in_specs=in_specs,
        out_specs=[whole(o.shape) for o in outs],
        scratch_shapes=scratch,
        compiler_params=pltpu.CompilerParams(vmem_limit_bytes=LIMIT),
        cost_estimate=pl.CostEstimate(
            flops=int(us * 8e8), bytes_accessed=int(us * 1e6), transcendentals=0
        ),
    )(*args)


def struct(shape, dtype=BF):
    return jax.ShapeDtypeStruct(shape, dtype)


def write_rows(value, head, place, out_ref, stage_ref):
    for frame in range(2):
        stage_ref[head, pl.ds(frame, ROWS, stride=2), :] = value[frame * ROWS : (frame + 1) * ROWS]
    out_ref[:, head, :, place] = stage_ref[head].reshape(4, 2, 8, 128).astype(BF)


def write_columns(tile_of, out_ref, stage_ref, place):
    lane = lax.broadcasted_iota(jnp.int32, (1, 128), 1)
    for tile in range(8):
        first, second = tile_of(tile)
        even = jnp.where(lane < HEAD, first, pltpu.roll(second, HEAD, 1))
        odd = jnp.where(lane < HEAD, pltpu.roll(first, HEAD, 1), second)
        write_rows(even, 2 * tile, place, out_ref, stage_ref)
        write_rows(odd, 2 * tile + 1, place, out_ref, stage_ref)


def write_pairs(low, high, out_ref, stage_ref, place):
    lane = lax.broadcasted_iota(jnp.int32, (1, 128), 1)
    for tile in range(8):
        for col, (a, b) in enumerate(zip(low(tile), high(tile))):
            even = jnp.where(lane < HEAD, a, pltpu.roll(b, HEAD, 1))
            odd = jnp.where(lane < HEAD, pltpu.roll(a, HEAD, 1), b)
            write_rows(even, 2 * tile, place + col, out_ref, stage_ref)
            write_rows(odd, 2 * tile + 1, place + col, out_ref, stage_ref)


def heads_of(in_ref, tile, place):
    even = in_ref[:, 2 * tile, :, place].astype(F32).reshape(2 * ROWS, 128)
    odd = in_ref[:, 2 * tile + 1, :, place].astype(F32).reshape(2 * ROWS, 128)
    lane = lax.broadcasted_iota(jnp.int32, (1, 128), 1)
    low = jnp.where(lane < HEAD, even, pltpu.roll(odd, HEAD, 1))
    high = jnp.where(lane < HEAD, pltpu.roll(even, HEAD, 1), odd)
    return low, high


def frame_rows(values, tile, stage_ref):
    for col in range(2):
        stage_ref[2 * tile + col] = values[col]
    for frame in range(2):
        yield frame, [stage_ref[2 * tile + col, pl.ds(frame, ROWS, stride=2), :] for col in range(2)]


def store_tokens(values, tile, target, stage_ref):
    for frame, cols in frame_rows(values, tile, stage_ref):
        target[frame * ROWS : (frame + 1) * ROWS, :, tile * 128 : (tile + 1) * 128] = jnp.stack(
            cols, axis=1
        ).astype(BF)


def tiles_of(ref):
    return lambda tile: [
        ref[:, col, tile * 128 : (tile + 1) * 128].astype(F32) for col in range(2)
    ]


def pack_body(q_ref, k_ref, v_ref, out_ref, stage_ref):
    write_columns(tiles_of(q_ref), out_ref, stage_ref, 0)
    write_pairs(tiles_of(k_ref), tiles_of(v_ref), out_ref, stage_ref, 1)


def extend(own_ref, near_ref, ext_ref, reverse):
    row = lax.broadcasted_iota(jnp.int32, (2 * ROWS, 1), 0) % ROWS
    for part, ref in enumerate((own_ref, near_ref)):
        first = 2 * part if reverse else 2 - 2 * part
        for col in range(4):
            value = ref[col].astype(F32).reshape(2 * ROWS, -1)
            up = jnp.where(row == 0, 0.0, pltpu.roll(value, 1, 0))
            down = jnp.where(row == ROWS - 1, 0.0, pltpu.roll(value, 2 * ROWS - 1, 0))
            for shift, moved in enumerate((up, value, down)):
                ext_ref[shift, col, first : first + 2] = moved.astype(BF).reshape(2, ROWS, -1)


def conv_step(own_ref, near_ref, taps_ref, ext_ref, acc_ref, reverse):
    step = pl.program_id(0)
    lag = step // 3
    shift = step % 3

    @pl.when(step == 0)
    def _():
        extend(own_ref, near_ref, ext_ref, reverse)
        acc_ref[...] = own_ref[1:3].astype(F32).reshape(4 * ROWS, -1)

    if reverse:
        lag = 2 - lag
        shift = 2 - shift
    total = None
    for b in range(3):
        col = 2 - b if reverse else b
        window = ext_ref[shift, col : col + 2, pl.ds(lag, 2)].reshape(4 * ROWS, -1)
        part = dot(window, taps_ref[0, 0, b], NT if reverse else NN)
        total = part if total is None else total + part
    acc_ref[...] += total


def conv_body(own_ref, near_ref, taps_ref, out_ref, ext_ref, acc_ref):
    conv_step(own_ref, near_ref, taps_ref, ext_ref, acc_ref, False)

    @pl.when(pl.program_id(0) == 8)
    def _():
        out_ref[...] = acc_ref[...].astype(BF)


def adjoint_body(own_ref, near_ref, taps_ref, proj_ref, out_ref, ext_ref, acc_ref, stage_ref):
    conv_step(own_ref, near_ref, taps_ref, ext_ref, acc_ref, True)

    @pl.when(pl.program_id(0) == 8)
    def _():
        grad = acc_ref[...].astype(BF)

        def tile_of(tile):
            value = dot(grad, proj_ref[tile * 128 : (tile + 1) * 128, :], NT)
            return value[: 2 * ROWS], value[2 * ROWS :]

        write_columns(tile_of, out_ref, stage_ref, 0)


def project_body(in_ref, proj_ref, out_ref, att_ref, stage_ref):
    for tile in range(8):
        for frame, cols in frame_rows(heads_of(in_ref, tile, 0), tile, stage_ref):
            for col in range(2):
                row = (col * 2 + frame) * ROWS
                att_ref[row : row + ROWS, tile * 128 : (tile + 1) * 128] = cols[col].astype(BF)
    out_ref[...] = dot(att_ref[...], proj_ref[...]).astype(BF)


def unpack_body(in_ref, gq_ref, gk_ref, gv_ref, stage_ref):
    for tile in range(8):
        store_tokens(heads_of(in_ref, tile, 0), tile, gq_ref, stage_ref.at[0])
        first = heads_of(in_ref, tile, 1)
        second = heads_of(in_ref, tile, 2)
        store_tokens((first[0], second[0]), tile, gk_ref, stage_ref.at[1])
        store_tokens((first[1], second[1]), tile, gv_ref, stage_ref.at[2])


def join_columns(value, out_ref, base, roll_low):
    lane = lax.broadcasted_iota(jnp.int32, (1, 128), 1)
    for x in range(4):
        first = value[x * 128 : x * 128 + 64]
        second = value[x * 128 + 64 : (x + 1) * 128]
        if roll_low:
            first = pltpu.roll(first, HEAD, 1)
        else:
            second = pltpu.roll(second, HEAD, 1)
        out_ref[pl.ds(pl.multiple_of(base + x * 64, 64), 64), :] = jnp.where(
            lane < HEAD, first, second
        ).astype(BF)


def split_columns(value, out_ref, group, high):
    lane = lax.broadcasted_iota(jnp.int32, (1, 128), 1)
    keep = lane >= HEAD if high else lane < HEAD
    moved = pltpu.roll(value, HEAD, 1)
    first, second = (moved, value) if high else (value, moved)
    out_ref[group * 128 : group * 128 + 64, :] = jnp.where(keep, first, 0.0).astype(BF)
    out_ref[group * 128 + 64 : (group + 1) * 128, :] = jnp.where(keep, second, 0.0).astype(BF)


def forward_body(number, first, last, *refs):
    refs = list(refs)
    kv_refs = [refs.pop(0) for _ in range(number)]
    source_ref = refs.pop(0)
    if not first:
        seed_ref = refs.pop(0)
    if last:
        do_ref = refs.pop(0)
        att_ref, stat_ref, grad_ref, kv_ref, max_ref, acc_ref, sems = refs
        query_ref = source_ref
    elif first:
        query_ref, state_ref, kv_ref, max_ref, acc_ref, sems = refs
    else:
        state_ref, kv_ref, max_ref, acc_ref, sems = refs
        query_ref = source_ref
    lane = lax.broadcasted_iota(jnp.int32, (1, 128), 1)
    one = jnp.ones((), BF)
    copies = [
        pltpu.make_async_copy(kv_refs[i], kv_ref.at[:, :, i], sems.at[i]) for i in range(number)
    ]
    for copy in copies:
        copy.start()
    for group in range(16):
        rows = slice(group * 8, (group + 1) * 8)
        if first:
            value = source_ref[rows].astype(F32).reshape(64, 128) * HEAD**-0.5
            split_columns(value, query_ref, group, False)
        if last:
            split_columns(do_ref[rows].astype(F32).reshape(64, 128), grad_ref, group, True)
    for copy in copies:
        copy.wait()

    def per_block(block, _):
        start = block * TOK
        rows = pl.ds(pl.multiple_of(start, TOK), TOK)
        if first:
            max_ref[...] = jnp.full(max_ref.shape, NEGATIVE, F32)
            acc_ref[...] = jnp.zeros(acc_ref.shape, F32)
        else:
            max_ref[...] = jnp.broadcast_to(seed_ref[rows, 1:2], max_ref.shape)
            acc_ref[...] = seed_ref[rows, :]

        def update(part, scores, keys):
            before = max_ref[part, :]
            high = jnp.max(scores, axis=1, keepdims=True)
            after = jnp.maximum(before, jnp.broadcast_to(high, before.shape))
            shift = jnp.concatenate([after] * (scores.shape[1] // 128), axis=1)
            weights = jnp.exp(scores - shift).astype(BF)
            moved = dot(weights, jnp.where(lane < HEAD, one, keys))
            acc_ref[part, :] = acc_ref[part, :] * jnp.exp(before - after) + moved
            max_ref[part, :] = after

        def whole(index, _):
            keys = kv_ref[index].reshape(number * TOK, 128)
            update(slice(None), dot(query_ref[rows, :], keys, NT), keys)
            return 0

        lax.fori_loop(0, block, whole, 0)
        for half in range(2):
            count = TOK - 256 * half
            query = query_ref[pl.ds(pl.multiple_of(start + half * 256, 256), count), :]
            keys = kv_ref[block, 2 * half : 2 * half + 2].reshape(number * 256, 128)
            row = lax.broadcasted_iota(jnp.int32, (count, 1), 0)
            key = lax.broadcasted_iota(jnp.int32, (1, number * 256), 1)
            hidden = row // 128 * 2 + row % 2 < key // (number * 128) * 2 + key % 2
            scores = jnp.where(hidden, NEGATIVE, dot(query, keys, NT))
            update(slice(half * 256, TOK), scores, keys)
        acc = acc_ref[...]
        if not last:
            state_ref[rows, :] = jnp.where(lane == 1, max_ref[...], acc)
            return 0
        total = acc[:, 0:1]
        att = (acc / total).astype(BF).astype(F32)
        delta = jnp.sum(att * grad_ref[rows, :].astype(F32), axis=1, keepdims=True)
        logsum = max_ref[:, 0:1] + jnp.log(total)
        stat_ref[:, rows] = jnp.where(lane == 0, logsum, delta).T[0:8, :]
        join_columns(att, att_ref, block * 256, True)
        return 0

    lax.fori_loop(0, 4, per_block, 0)


def backward_body(first, last, same_ref, other_ref, query_ref, grad_ref, stat_ref, *refs):
    refs = list(refs)
    seed_ref = None if first else refs.pop(0)
    same_out, other_out, dq_out, kv_ref, turned_ref, acc_ref, dq_ref = refs
    eye = (
        lax.broadcasted_iota(jnp.int32, (128, 128), 0)
        == lax.broadcasted_iota(jnp.int32, (128, 128), 1)
    ).astype(BF)
    kv_ref[:, :, 0] = same_ref[...]
    kv_ref[:, :, 1] = other_ref[...]
    dq_ref[...] = jnp.zeros(dq_ref.shape, F32) if first else seed_ref[...]

    def per_keys(block, _):
        turned_ref[...] = dot(eye, kv_ref[block].reshape(2 * TOK, 128), NT).astype(BF)
        acc_ref[...] = jnp.zeros(acc_ref.shape, F32)

        def pairs(start, count, part, masked):
            rows = pl.ds(pl.multiple_of(start, 128), count)
            query = query_ref[rows, :]
            grad = grad_ref[rows, :]
            stats = stat_ref[:, rows]
            keys = kv_ref[block].reshape(2 * TOK, 128)[part]
            probs = jnp.exp(dot(keys, query, NT) - stats[0:1, :])
            if masked:
                key = lax.broadcasted_iota(jnp.int32, (keys.shape[0], 1), 0)
                row = lax.broadcasted_iota(jnp.int32, (1, count), 1)
                hidden = key // 256 * 2 + key % 2 > row // 128 * 2 + row % 2
                probs = jnp.where(hidden, 0.0, probs)
            inner = (probs * (dot(keys, grad, NT) - stats[1:2, :])).astype(BF)
            acc_ref[part, :] += dot(inner, query) + dot(probs.astype(BF), grad)
            dq_ref[:, rows] += dot(turned_ref[:, part], inner)

        def whole(later, _):
            pairs(later * TOK, TOK, slice(0, 2 * TOK), False)
            return 0

        lax.fori_loop(block + 1, 4, whole, 0)
        pairs(block * TOK, TOK, slice(0, TOK), True)
        pairs(block * TOK + 256, 256, slice(TOK, 2 * TOK), True)
        total = acc_ref[...].astype(BF).reshape(4, 2, 128, 128)
        same_out[block] = total[:, 0]
        other_out[block] = total[:, 1]
        return 0

    lax.fori_loop(0, 4, per_keys, 0)
    if last:
        for block in range(4):
            value = (dq_ref[:, block * TOK : (block + 1) * TOK] * HEAD**-0.5).T
            join_columns(value, dq_out, block * 256, False)
    else:
        dq_out[...] = dq_ref[...]


def shift_y(value, steps):
    return lax.ppermute(value, "y", [(i, (i + steps) % 4) for i in range(4)])


def swap_core(value):
    return lax.ppermute(value, "c", [(0, 1), (1, 0)])


def halo(own, forward):
    step = 1 if forward else -1

    def turn(value, cols):
        pairs = [(i, (i + cols) % 8) for i in range(8)]
        return lax.ppermute(value, ("z", "c"), pairs)

    left = turn(own[1:], 1)
    right = turn(own[:1], -1)
    wide = jnp.concatenate([left, own, right], axis=0)
    frames = [(t, t + step) for t in range(16) if 0 <= t + step < 16]
    return wide, lax.ppermute(wide, ("y", "x"), frames)


def exchange_all(value):
    split = value.reshape(128, -1, 128)
    return lax.all_to_all(split, AXES, split_axis=0, concat_axis=0, tiled=True)


def columns_first(array):
    return array.transpose(2, 0, 1, 3)


def flat(array):
    return array.reshape(2 * ROWS, 2, -1)


def tokens_back(array):
    return array.reshape(2, 2, ROWS, -1).transpose(1, 2, 0, 3)


def shards(queries, key_rows, value_rows, out_proj, conv_taps, cotangent):
    channels = out_proj.shape[1]
    stage = pltpu.VMEM((16, 2 * ROWS, 128), F32)
    taps_spec = pl.BlockSpec((1, 1, 3, channels, channels), lambda t: (t // 3, t % 3, 0, 0, 0))
    conv_scratch = [
        pltpu.VMEM((3, 4, 4, ROWS, channels), BF),
        pltpu.VMEM((4 * ROWS, channels), F32),
    ]
    grouped = (4, 4, 128, 128)

    near = halo(columns_first(cotangent), False)
    (packed,) = kernel_call(
        pack_body,
        [struct((4, 16, 2, 3, 8, 128))],
        [stage],
        (flat(queries), flat(key_rows), flat(value_rows)),
        us=4.0,
    )
    packed = exchange_all(packed)
    (grad,) = kernel_call(
        adjoint_body,
        [struct((4, 16, 2, 1, 8, 128))],
        [*conv_scratch, stage],
        (*near, conv_taps, out_proj),
        grid=(9,),
        specs={2: taps_spec},
        us=12.0,
    )
    packed, grad = lax.optimization_barrier((packed, grad))
    source = packed[:, :8]
    kv_same = {0: packed[:, 8:].reshape(grouped)}
    for steps in (1, 3, 2):
        kv_same[steps] = shift_y(kv_same[0], steps)
    kv_other = {steps: swap_core(kv_same[steps]) for steps in (0, 1, 3, 2)}
    grad = exchange_all(grad)

    def attend(arrays, extra, outs, us, first=False, last=False):
        number = len(arrays)
        return kernel_call(
            functools.partial(forward_body, number, first, last),
            outs,
            [
                pltpu.VMEM((4, 4, number, 128, 128), BF),
                pltpu.VMEM((TOK, 128), F32),
                pltpu.VMEM((TOK, 128), F32),
                pltpu.SemaphoreType.DMA((number,)),
            ],
            (*arrays, *extra),
            specs={index: pl.BlockSpec(memory_space=pl.ANY) for index in range(number)},
            us=us,
        )

    state = struct((SPAN, 128), F32)
    query, seed = attend(
        [kv_same[0], kv_other[0]], (source,), [struct((SPAN, 128)), state], 10.0, True
    )
    rest = [kv_same[i] for i in (1, 3, 2)] + [kv_other[i] for i in (1, 3, 2)]
    att, stats, grad = attend(
        rest,
        (query, seed, grad),
        [struct((SPAN // 2, 128)), struct((8, SPAN), F32), struct((SPAN, 128))],
        25.0,
        last=True,
    )
    att = exchange_all(att).reshape(4, 16, 2, 1, 8, 128)

    seed = None
    total = None
    for steps in (2, 1, 3, 0):
        last = steps == 0
        same, other, seed = kernel_call(
            functools.partial(backward_body, seed is None, last),
            [
                struct(grouped),
                struct(grouped),
                struct((SPAN // 2, 128)) if last else struct((128, SPAN), F32),
            ],
            [
                pltpu.VMEM((4, 4, 2, 128, 128), BF),
                pltpu.VMEM((128, 2 * TOK), BF),
                pltpu.VMEM((2 * TOK, 128), F32),
                pltpu.VMEM((128, SPAN), F32),
            ],
            (kv_same[steps], kv_other[steps], query, grad, stats)
            + (() if seed is None else (seed,)),
            us=16.0,
        )
        joined = same.astype(F32) + swap_core(other).astype(F32)
        if not last:
            joined = shift_y(joined.astype(BF), 4 - steps).astype(F32)
        total = joined if total is None else total + joined
    (projected,) = kernel_call(
        project_body,
        [struct((4 * ROWS, channels))],
        [pltpu.VMEM((4 * ROWS, 1024), BF), stage],
        (att, out_proj),
        us=3.0,
    )
    near = halo(projected.reshape(2, 2, ROWS, channels), True)
    (conv,) = kernel_call(
        conv_body,
        [struct((4 * ROWS, channels))],
        conv_scratch,
        (*near, conv_taps),
        grid=(9,),
        specs={2: taps_spec},
        us=10.0,
    )
    grads = jnp.concatenate(
        [seed.reshape(128, 8, 128), total.astype(BF).reshape(128, 16, 128)], axis=1
    )
    grads = exchange_all(grads).reshape(4, 16, 2, 3, 8, 128)
    grads = kernel_call(
        unpack_body,
        [struct((2 * ROWS, 2, 1024))] * 3,
        [pltpu.VMEM((3, 16, 2 * ROWS, 128), F32)],
        (grads,),
        us=4.0,
    )
    return (tokens_back(conv), *(g.reshape(queries.shape) for g in grads))


def solution(mesh):
    grid = Mesh(mesh.devices.reshape(4, 4, 4, 2), AXES)
    spec = P(("y", "x"), None, ("z", "c"), None)
    return jax.shard_map(
        shards,
        mesh=grid,
        in_specs=(spec, spec, spec, P(), P(), spec),
        out_specs=(spec,) * 4,
        check_vma=False,
    )
```

```python
import functools

import jax
import jax.numpy as jnp
from jax import lax
from jax.experimental import pallas as pl
from jax.experimental.pallas import tpu as pltpu
from jax.sharding import Mesh, PartitionSpec as P


HEAD = 64
NEGATIVE = -1e30
BF = jnp.bfloat16
F32 = jnp.float32
NN = (((1,), (0,)), ((), ()))
NT = (((1,), (1,)), ((), ()))
AXES = ("y", "x", "z", "c")
ROWS = 32
TOK = 512
SPAN = 4 * TOK
LIMIT = 60 * 2**20


def dot(a, b, dims=NN):
    return lax.dot_general(a, b, dims, preferred_element_type=F32)


def kernel_call(body, outs, scratch, args, grid=(1,), specs=None, us=1.0):
    def whole(shape):
        rank = len(shape)
        return pl.BlockSpec(shape, lambda *_: (0,) * rank)

    in_specs = [whole(a.shape) for a in args]
    for index, spec in (specs or {}).items():
        in_specs[index] = spec
    return pl.pallas_call(
        body,
        out_shape=outs,
        grid=grid,
        in_specs=in_specs,
        out_specs=[whole(o.shape) for o in outs],
        scratch_shapes=scratch,
        compiler_params=pltpu.CompilerParams(vmem_limit_bytes=LIMIT),
        cost_estimate=pl.CostEstimate(
            flops=int(us * 8e8), bytes_accessed=int(us * 1e6), transcendentals=0
        ),
    )(*args)


def struct(shape, dtype=BF):
    return jax.ShapeDtypeStruct(shape, dtype)


def write_rows(value, head, place, out_ref, stage_ref):
    for frame in range(2):
        stage_ref[head, pl.ds(frame, ROWS, stride=2), :] = value[frame * ROWS : (frame + 1) * ROWS]
    out_ref[:, head, :, place] = stage_ref[head].reshape(4, 2, 8, 128).astype(BF)


def write_columns(tile_of, out_ref, stage_ref, place):
    lane = lax.broadcasted_iota(jnp.int32, (1, 128), 1)
    for tile in range(8):
        first, second = tile_of(tile)
        even = jnp.where(lane < HEAD, first, pltpu.roll(second, HEAD, 1))
        odd = jnp.where(lane < HEAD, pltpu.roll(first, HEAD, 1), second)
        write_rows(even, 2 * tile, place, out_ref, stage_ref)
        write_rows(odd, 2 * tile + 1, place, out_ref, stage_ref)


def write_pairs(low, high, out_ref, stage_ref, place):
    lane = lax.broadcasted_iota(jnp.int32, (1, 128), 1)
    for tile in range(8):
        for col, (a, b) in enumerate(zip(low(tile), high(tile))):
            even = jnp.where(lane < HEAD, a, pltpu.roll(b, HEAD, 1))
            odd = jnp.where(lane < HEAD, pltpu.roll(a, HEAD, 1), b)
            write_rows(even, 2 * tile, place + col, out_ref, stage_ref)
            write_rows(odd, 2 * tile + 1, place + col, out_ref, stage_ref)


def heads_of(in_ref, tile, place):
    even = in_ref[:, 2 * tile, :, place].astype(F32).reshape(2 * ROWS, 128)
    odd = in_ref[:, 2 * tile + 1, :, place].astype(F32).reshape(2 * ROWS, 128)
    lane = lax.broadcasted_iota(jnp.int32, (1, 128), 1)
    low = jnp.where(lane < HEAD, even, pltpu.roll(odd, HEAD, 1))
    high = jnp.where(lane < HEAD, pltpu.roll(even, HEAD, 1), odd)
    return low, high


def frame_rows(values, tile, stage_ref):
    for col in range(2):
        stage_ref[2 * tile + col] = values[col]
    for frame in range(2):
        yield frame, [stage_ref[2 * tile + col, pl.ds(frame, ROWS, stride=2), :] for col in range(2)]


def store_tokens(values, tile, target, stage_ref):
    for frame, cols in frame_rows(values, tile, stage_ref):
        target[frame * ROWS : (frame + 1) * ROWS, :, tile * 128 : (tile + 1) * 128] = jnp.stack(
            cols, axis=1
        ).astype(BF)


def tiles_of(ref):
    return lambda tile: [
        ref[:, col, tile * 128 : (tile + 1) * 128].astype(F32) for col in range(2)
    ]


def pack_body(q_ref, k_ref, v_ref, out_ref, stage_ref):
    write_columns(tiles_of(q_ref), out_ref, stage_ref, 0)
    write_pairs(tiles_of(k_ref), tiles_of(v_ref), out_ref, stage_ref, 1)


def extend(own_ref, near_ref, ext_ref, reverse):
    row = lax.broadcasted_iota(jnp.int32, (2 * ROWS, 1), 0) % ROWS
    for part, ref in enumerate((own_ref, near_ref)):
        first = 2 * part if reverse else 2 - 2 * part
        for col in range(4):
            value = ref[col].astype(F32).reshape(2 * ROWS, -1)
            up = jnp.where(row == 0, 0.0, pltpu.roll(value, 1, 0))
            down = jnp.where(row == ROWS - 1, 0.0, pltpu.roll(value, 2 * ROWS - 1, 0))
            for shift, moved in enumerate((up, value, down)):
                ext_ref[shift, col, first : first + 2] = moved.astype(BF).reshape(2, ROWS, -1)


def conv_step(own_ref, near_ref, taps_ref, ext_ref, acc_ref, reverse):
    step = pl.program_id(0)
    lag = step // 3
    shift = step % 3

    @pl.when(step == 0)
    def _():
        extend(own_ref, near_ref, ext_ref, reverse)
        acc_ref[...] = own_ref[1:3].astype(F32).reshape(4 * ROWS, -1)

    if reverse:
        lag = 2 - lag
        shift = 2 - shift
    total = None
    for b in range(3):
        col = 2 - b if reverse else b
        window = ext_ref[shift, col : col + 2, pl.ds(lag, 2)].reshape(4 * ROWS, -1)
        part = dot(window, taps_ref[0, 0, b], NT if reverse else NN)
        total = part if total is None else total + part
    acc_ref[...] += total


def conv_body(own_ref, near_ref, taps_ref, out_ref, ext_ref, acc_ref):
    conv_step(own_ref, near_ref, taps_ref, ext_ref, acc_ref, False)

    @pl.when(pl.program_id(0) == 8)
    def _():
        out_ref[...] = acc_ref[...].astype(BF)


def adjoint_body(own_ref, near_ref, taps_ref, proj_ref, out_ref, ext_ref, acc_ref, stage_ref):
    conv_step(own_ref, near_ref, taps_ref, ext_ref, acc_ref, True)

    @pl.when(pl.program_id(0) == 8)
    def _():
        grad = acc_ref[...].astype(BF)

        def tile_of(tile):
            value = dot(grad, proj_ref[tile * 128 : (tile + 1) * 128, :], NT)
            return value[: 2 * ROWS], value[2 * ROWS :]

        write_columns(tile_of, out_ref, stage_ref, 0)


def project_body(in_ref, proj_ref, out_ref, att_ref, stage_ref):
    for tile in range(8):
        for frame, cols in frame_rows(heads_of(in_ref, tile, 0), tile, stage_ref):
            for col in range(2):
                row = (col * 2 + frame) * ROWS
                att_ref[row : row + ROWS, tile * 128 : (tile + 1) * 128] = cols[col].astype(BF)
    out_ref[...] = dot(att_ref[...], proj_ref[...]).astype(BF)


def unpack_body(in_ref, gq_ref, gk_ref, gv_ref, stage_ref):
    for tile in range(8):
        store_tokens(heads_of(in_ref, tile, 0), tile, gq_ref, stage_ref.at[0])
        first = heads_of(in_ref, tile, 1)
        second = heads_of(in_ref, tile, 2)
        store_tokens((first[0], second[0]), tile, gk_ref, stage_ref.at[1])
        store_tokens((first[1], second[1]), tile, gv_ref, stage_ref.at[2])


def join_columns(value, out_ref, base, roll_low):
    lane = lax.broadcasted_iota(jnp.int32, (1, 128), 1)
    for x in range(4):
        first = value[x * 128 : x * 128 + 64]
        second = value[x * 128 + 64 : (x + 1) * 128]
        if roll_low:
            first = pltpu.roll(first, HEAD, 1)
        else:
            second = pltpu.roll(second, HEAD, 1)
        out_ref[pl.ds(pl.multiple_of(base + x * 64, 64), 64), :] = jnp.where(
            lane < HEAD, first, second
        ).astype(BF)


def split_columns(value, out_ref, group, high):
    lane = lax.broadcasted_iota(jnp.int32, (1, 128), 1)
    keep = lane >= HEAD if high else lane < HEAD
    moved = pltpu.roll(value, HEAD, 1)
    first, second = (moved, value) if high else (value, moved)
    out_ref[group * 128 : group * 128 + 64, :] = jnp.where(keep, first, 0.0).astype(BF)
    out_ref[group * 128 + 64 : (group + 1) * 128, :] = jnp.where(keep, second, 0.0).astype(BF)


def forward_body(number, first, last, *refs):
    refs = list(refs)
    kv_refs = [refs.pop(0) for _ in range(number)]
    source_ref = refs.pop(0)
    if not first:
        seed_ref = refs.pop(0)
    if last:
        do_ref = refs.pop(0)
        att_ref, stat_ref, grad_ref, kv_ref, max_ref, acc_ref, sems = refs
        query_ref = source_ref
    elif first:
        query_ref, state_ref, kv_ref, max_ref, acc_ref, sems = refs
    else:
        state_ref, kv_ref, max_ref, acc_ref, sems = refs
        query_ref = source_ref
    lane = lax.broadcasted_iota(jnp.int32, (1, 128), 1)
    one = jnp.ones((), BF)
    copies = [
        pltpu.make_async_copy(kv_refs[i], kv_ref.at[:, :, i], sems.at[i]) for i in range(number)
    ]
    for copy in copies:
        copy.start()
    for group in range(16):
        rows = slice(group * 8, (group + 1) * 8)
        if first:
            value = source_ref[rows].astype(F32).reshape(64, 128) * HEAD**-0.5
            split_columns(value, query_ref, group, False)
        if last:
            split_columns(do_ref[rows].astype(F32).reshape(64, 128), grad_ref, group, True)
    for copy in copies:
        copy.wait()

    def per_block(block, _):
        start = block * TOK
        rows = pl.ds(pl.multiple_of(start, TOK), TOK)
        if first:
            max_ref[...] = jnp.full(max_ref.shape, NEGATIVE, F32)
            acc_ref[...] = jnp.zeros(acc_ref.shape, F32)
        else:
            max_ref[...] = jnp.broadcast_to(seed_ref[rows, 1:2], max_ref.shape)
            acc_ref[...] = seed_ref[rows, :]

        def update(part, scores, keys):
            before = max_ref[part, :]
            high = jnp.max(scores, axis=1, keepdims=True)
            after = jnp.maximum(before, jnp.broadcast_to(high, before.shape))
            shift = jnp.concatenate([after] * (scores.shape[1] // 128), axis=1)
            weights = jnp.exp(scores - shift).astype(BF)
            moved = dot(weights, jnp.where(lane < HEAD, one, keys))
            acc_ref[part, :] = acc_ref[part, :] * jnp.exp(before - after) + moved
            max_ref[part, :] = after

        def whole(index, _):
            keys = kv_ref[index].reshape(number * TOK, 128)
            update(slice(None), dot(query_ref[rows, :], keys, NT), keys)
            return 0

        lax.fori_loop(0, block, whole, 0)
        width = 128 if number == 2 else 256
        for part in range(TOK // width):
            count = TOK - width * part
            query = query_ref[pl.ds(pl.multiple_of(start + part * width, width), count), :]
            each = width // 128
            keys = kv_ref[block, each * part : each * (part + 1)].reshape(number * width, 128)
            row = lax.broadcasted_iota(jnp.int32, (count, 1), 0)
            key = lax.broadcasted_iota(jnp.int32, (1, number * width), 1)
            hidden = row // 128 * 2 + row % 2 < key // (number * 128) * 2 + key % 2
            scores = jnp.where(hidden, NEGATIVE, dot(query, keys, NT))
            update(slice(part * width, TOK), scores, keys)
        acc = acc_ref[...]
        if not last:
            state_ref[rows, :] = jnp.where(lane == 1, max_ref[...], acc)
            return 0
        total = acc[:, 0:1]
        att = (acc / total).astype(BF).astype(F32)
        delta = jnp.sum(att * grad_ref[rows, :].astype(F32), axis=1, keepdims=True)
        logsum = max_ref[:, 0:1] + jnp.log(total)
        stat_ref[:, rows] = jnp.where(lane == 0, logsum, delta).T[0:8, :]
        join_columns(att, att_ref, block * 256, True)
        return 0

    lax.fori_loop(0, 4, per_block, 0)


def backward_body(first, last, same_ref, other_ref, query_ref, grad_ref, stat_ref, *refs):
    refs = list(refs)
    seed_ref = None if first else refs.pop(0)
    same_out, other_out, dq_out, kv_ref, turned_ref, acc_ref, dq_ref = refs
    eye = (
        lax.broadcasted_iota(jnp.int32, (128, 128), 0)
        == lax.broadcasted_iota(jnp.int32, (128, 128), 1)
    ).astype(BF)
    kv_ref[:, :, 0] = same_ref[...]
    kv_ref[:, :, 1] = other_ref[...]
    dq_ref[...] = jnp.zeros(dq_ref.shape, F32) if first else seed_ref[...]

    def per_keys(block, _):
        turned_ref[...] = dot(eye, kv_ref[block].reshape(2 * TOK, 128), NT).astype(BF)
        acc_ref[...] = jnp.zeros(acc_ref.shape, F32)

        def pairs(start, count, part, masked):
            rows = pl.ds(pl.multiple_of(start, 128), count)
            query = query_ref[rows, :]
            grad = grad_ref[rows, :]
            stats = stat_ref[:, rows]
            keys = kv_ref[block].reshape(2 * TOK, 128)[part]
            probs = jnp.exp(dot(keys, query, NT) - stats[0:1, :])
            if masked:
                key = lax.broadcasted_iota(jnp.int32, (keys.shape[0], 1), 0)
                row = lax.broadcasted_iota(jnp.int32, (1, count), 1)
                hidden = key // 256 * 2 + key % 2 > row // 128 * 2 + row % 2
                probs = jnp.where(hidden, 0.0, probs)
            inner = (probs * (dot(keys, grad, NT) - stats[1:2, :])).astype(BF)
            acc_ref[part, :] += dot(inner, query) + dot(probs.astype(BF), grad)
            dq_ref[:, rows] += dot(turned_ref[:, part], inner)

        def whole(later, _):
            pairs(later * TOK, TOK, slice(0, 2 * TOK), False)
            return 0

        lax.fori_loop(block + 1, 4, whole, 0)
        pairs(block * TOK, TOK, slice(0, TOK), True)
        pairs(block * TOK + 256, 256, slice(TOK, 2 * TOK), True)
        total = acc_ref[...].astype(BF).reshape(4, 2, 128, 128)
        same_out[block] = total[:, 0]
        other_out[block] = total[:, 1]
        return 0

    lax.fori_loop(0, 4, per_keys, 0)
    if last:
        for block in range(4):
            value = (dq_ref[:, block * TOK : (block + 1) * TOK] * HEAD**-0.5).T
            join_columns(value, dq_out, block * 256, False)
    else:
        dq_out[...] = dq_ref[...]


def shift_y(value, steps):
    return lax.ppermute(value, "y", [(i, (i + steps) % 4) for i in range(4)])


def swap_core(value):
    return lax.ppermute(value, "c", [(0, 1), (1, 0)])


def halo(own, forward):
    step = 1 if forward else -1

    def turn(value, cols):
        pairs = [(i, (i + cols) % 8) for i in range(8)]
        return lax.ppermute(value, ("z", "c"), pairs)

    left = turn(own[1:], 1)
    right = turn(own[:1], -1)
    wide = jnp.concatenate([left, own, right], axis=0)
    frames = [(t, t + step) for t in range(16) if 0 <= t + step < 16]
    return wide, lax.ppermute(wide, ("y", "x"), frames)


def exchange_all(value):
    split = value.reshape(128, -1, 128)
    return lax.all_to_all(split, AXES, split_axis=0, concat_axis=0, tiled=True)


def columns_first(array):
    return array.transpose(2, 0, 1, 3)


def flat(array):
    return array.reshape(2 * ROWS, 2, -1)


def tokens_back(array):
    return array.reshape(2, 2, ROWS, -1).transpose(1, 2, 0, 3)


def shards(queries, key_rows, value_rows, out_proj, conv_taps, cotangent):
    channels = out_proj.shape[1]
    stage = pltpu.VMEM((16, 2 * ROWS, 128), F32)
    taps_spec = pl.BlockSpec((1, 1, 3, channels, channels), lambda t: (t // 3, t % 3, 0, 0, 0))
    conv_scratch = [
        pltpu.VMEM((3, 4, 4, ROWS, channels), BF),
        pltpu.VMEM((4 * ROWS, channels), F32),
    ]
    grouped = (4, 4, 128, 128)

    near = halo(columns_first(cotangent), False)
    (packed,) = kernel_call(
        pack_body,
        [struct((4, 16, 2, 3, 8, 128))],
        [stage],
        (flat(queries), flat(key_rows), flat(value_rows)),
        us=4.0,
    )
    packed = exchange_all(packed)
    (grad,) = kernel_call(
        adjoint_body,
        [struct((4, 16, 2, 1, 8, 128))],
        [*conv_scratch, stage],
        (*near, conv_taps, out_proj),
        grid=(9,),
        specs={2: taps_spec},
        us=12.0,
    )
    packed, grad = lax.optimization_barrier((packed, grad))
    kv_same = {0: packed[:, 8:].reshape(grouped)}
    for steps in (1, 3, 2):
        kv_same[steps] = shift_y(kv_same[0], steps)
    kv_other = {steps: swap_core(kv_same[steps]) for steps in (0, 1, 3, 2)}
    grad = exchange_all(grad)

    def attend(arrays, extra, outs, us, first=False, last=False):
        number = len(arrays)
        specs = {index: pl.BlockSpec(memory_space=pl.ANY) for index in range(number)}
        if first:
            specs[number] = pl.BlockSpec((128, 8, 128), lambda *_: (0, 0, 0))
        return kernel_call(
            functools.partial(forward_body, number, first, last),
            outs,
            [
                pltpu.VMEM((4, 4, number, 128, 128), BF),
                pltpu.VMEM((TOK, 128), F32),
                pltpu.VMEM((TOK, 128), F32),
                pltpu.SemaphoreType.DMA((number,)),
            ],
            (*arrays, *extra),
            specs=specs,
            us=us,
        )

    state = struct((SPAN, 128), F32)
    query, seed = attend(
        [kv_same[0], kv_other[0]], (packed,), [struct((SPAN, 128)), state], 10.0, True
    )
    rest = [kv_same[i] for i in (1, 3, 2)] + [kv_other[i] for i in (1, 3, 2)]
    att, stats, grad = attend(
        rest,
        (query, seed, grad),
        [struct((SPAN // 2, 128)), struct((8, SPAN), F32), struct((SPAN, 128))],
        25.0,
        last=True,
    )
    att = exchange_all(att).reshape(4, 16, 2, 1, 8, 128)

    seed = None
    total = None
    for steps in (2, 1, 3, 0):
        last = steps == 0
        same, other, seed = kernel_call(
            functools.partial(backward_body, seed is None, last),
            [
                struct(grouped),
                struct(grouped),
                struct((SPAN // 2, 128)) if last else struct((128, SPAN), F32),
            ],
            [
                pltpu.VMEM((4, 4, 2, 128, 128), BF),
                pltpu.VMEM((128, 2 * TOK), BF),
                pltpu.VMEM((2 * TOK, 128), F32),
                pltpu.VMEM((128, SPAN), F32),
            ],
            (kv_same[steps], kv_other[steps], query, grad, stats)
            + (() if seed is None else (seed,)),
            us=16.0,
        )
        joined = same.astype(F32) + swap_core(other).astype(F32)
        if not last:
            joined = shift_y(joined.astype(BF), 4 - steps).astype(F32)
        total = joined if total is None else total + joined
    (projected,) = kernel_call(
        project_body,
        [struct((4 * ROWS, channels))],
        [pltpu.VMEM((4 * ROWS, 1024), BF), stage],
        (att, out_proj),
        us=3.0,
    )
    near = halo(projected.reshape(2, 2, ROWS, channels), True)
    (conv,) = kernel_call(
        conv_body,
        [struct((4 * ROWS, channels))],
        conv_scratch,
        (*near, conv_taps),
        grid=(9,),
        specs={2: taps_spec},
        us=10.0,
    )
    grads = jnp.concatenate(
        [seed.reshape(128, 8, 128), total.astype(BF).reshape(128, 16, 128)], axis=1
    )
    grads = exchange_all(grads).reshape(4, 16, 2, 3, 8, 128)
    grads = kernel_call(
        unpack_body,
        [struct((2 * ROWS, 2, 1024))] * 3,
        [pltpu.VMEM((3, 16, 2 * ROWS, 128), F32)],
        (grads,),
        us=4.0,
    )
    return (tokens_back(conv), *(g.reshape(queries.shape) for g in grads))


def solution(mesh):
    grid = Mesh(mesh.devices.reshape(4, 4, 4, 2), AXES)
    spec = P(("y", "x"), None, ("z", "c"), None)
    return jax.shard_map(
        shards,
        mesh=grid,
        in_specs=(spec, spec, spec, P(), P(), spec),
        out_specs=(spec,) * 4,
        check_vma=False,
    )
```

```python
import functools

import jax
import jax.numpy as jnp
from jax import lax
from jax.experimental import pallas as pl
from jax.experimental.pallas import tpu as pltpu
from jax.sharding import Mesh, PartitionSpec as P


HEAD = 64
NEGATIVE = -1e30
BF = jnp.bfloat16
F32 = jnp.float32
NN = (((1,), (0,)), ((), ()))
NT = (((1,), (1,)), ((), ()))
AXES = ("y", "x", "z", "c")
ROWS = 32
TOK = 512
SPAN = 4 * TOK
LIMIT = 60 * 2**20


def dot(a, b, dims=NN):
    return lax.dot_general(a, b, dims, preferred_element_type=F32)


def kernel_call(body, outs, scratch, args, grid=(1,), specs=None, us=1.0):
    def whole(shape):
        rank = len(shape)
        return pl.BlockSpec(shape, lambda *_: (0,) * rank)

    in_specs = [whole(a.shape) for a in args]
    for index, spec in (specs or {}).items():
        in_specs[index] = spec
    return pl.pallas_call(
        body,
        out_shape=outs,
        grid=grid,
        in_specs=in_specs,
        out_specs=[whole(o.shape) for o in outs],
        scratch_shapes=scratch,
        compiler_params=pltpu.CompilerParams(vmem_limit_bytes=LIMIT),
        cost_estimate=pl.CostEstimate(
            flops=int(us * 8e8), bytes_accessed=int(us * 1e6), transcendentals=0
        ),
    )(*args)


def struct(shape, dtype=BF):
    return jax.ShapeDtypeStruct(shape, dtype)


def write_rows(value, head, place, out_ref, stage_ref):
    for frame in range(2):
        stage_ref[head, pl.ds(frame, ROWS, stride=2), :] = value[frame * ROWS : (frame + 1) * ROWS]
    value = stage_ref[head, : 2 * ROWS]
    out_ref[:, head, :, place] = value.reshape(4, 2, 8, 128).astype(BF)


def write_columns(tile_of, out_ref, stage_ref, place):
    lane = lax.broadcasted_iota(jnp.int32, (1, 128), 1)
    for tile in range(8):
        first, second = tile_of(tile)
        even = jnp.where(lane < HEAD, first, pltpu.roll(second, HEAD, 1))
        odd = jnp.where(lane < HEAD, pltpu.roll(first, HEAD, 1), second)
        write_rows(even, 2 * tile, place, out_ref, stage_ref)
        write_rows(odd, 2 * tile + 1, place, out_ref, stage_ref)


def write_pairs(low, high, out_ref, stage_ref, place):
    lane = lax.broadcasted_iota(jnp.int32, (1, 128), 1)
    for tile in range(8):
        for col, (a, b) in enumerate(zip(low(tile), high(tile))):
            even = jnp.where(lane < HEAD, a, pltpu.roll(b, HEAD, 1))
            odd = jnp.where(lane < HEAD, pltpu.roll(a, HEAD, 1), b)
            write_rows(even, 2 * tile, place + col, out_ref, stage_ref)
            write_rows(odd, 2 * tile + 1, place + col, out_ref, stage_ref)


def heads_of(in_ref, tile, place):
    even = in_ref[:, 2 * tile, :, place].astype(F32).reshape(2 * ROWS, 128)
    odd = in_ref[:, 2 * tile + 1, :, place].astype(F32).reshape(2 * ROWS, 128)
    lane = lax.broadcasted_iota(jnp.int32, (1, 128), 1)
    low = jnp.where(lane < HEAD, even, pltpu.roll(odd, HEAD, 1))
    high = jnp.where(lane < HEAD, pltpu.roll(even, HEAD, 1), odd)
    return low, high


def frame_rows(values, tile, stage_ref):
    for col in range(2):
        stage_ref[2 * tile + col, : 2 * ROWS] = values[col]
    for frame in range(2):
        yield frame, [stage_ref[2 * tile + col, pl.ds(frame, ROWS, stride=2), :] for col in range(2)]


def store_tokens(values, tile, target, stage_ref):
    for frame, cols in frame_rows(values, tile, stage_ref):
        target[frame * ROWS : (frame + 1) * ROWS, :, tile * 128 : (tile + 1) * 128] = jnp.stack(
            cols, axis=1
        ).astype(BF)


def tiles_of(ref):
    return lambda tile: [
        ref[:, col, tile * 128 : (tile + 1) * 128].astype(F32) for col in range(2)
    ]


def pack_body(q_ref, k_ref, v_ref, out_ref, stage_ref):
    write_columns(tiles_of(q_ref), out_ref, stage_ref, 0)
    write_pairs(tiles_of(k_ref), tiles_of(v_ref), out_ref, stage_ref, 1)


def extend(own_ref, near_ref, ext_ref, reverse):
    row = lax.broadcasted_iota(jnp.int32, (2 * ROWS, 1), 0) % ROWS
    for part, ref in enumerate((own_ref, near_ref)):
        first = 2 * part if reverse else 2 - 2 * part
        for col in range(4):
            value = ref[col].astype(F32).reshape(2 * ROWS, -1)
            up = jnp.where(row == 0, 0.0, pltpu.roll(value, 1, 0))
            down = jnp.where(row == ROWS - 1, 0.0, pltpu.roll(value, 2 * ROWS - 1, 0))
            for shift, moved in enumerate((up, value, down)):
                ext_ref[shift, col, first : first + 2] = moved.astype(BF).reshape(2, ROWS, -1)


def conv_step(own_ref, near_ref, taps_ref, ext_ref, acc_ref, reverse):
    step = pl.program_id(0)
    lag = step // 3
    shift = step % 3

    @pl.when(step == 0)
    def _():
        extend(own_ref, near_ref, ext_ref, reverse)
        acc_ref[...] = own_ref[1:3].astype(F32).reshape(4 * ROWS, -1)

    if reverse:
        lag = 2 - lag
        shift = 2 - shift
    total = None
    for b in range(3):
        col = 2 - b if reverse else b
        window = ext_ref[shift, col : col + 2, pl.ds(lag, 2)].reshape(4 * ROWS, -1)
        part = dot(window, taps_ref[0, 0, b], NT if reverse else NN)
        total = part if total is None else total + part
    acc_ref[...] += total


def conv_body(own_ref, near_ref, taps_ref, out_ref, ext_ref, acc_ref):
    conv_step(own_ref, near_ref, taps_ref, ext_ref, acc_ref, False)

    @pl.when(pl.program_id(0) == 8)
    def _():
        out_ref[...] = acc_ref[...].astype(BF)


def adjoint_body(own_ref, near_ref, taps_ref, proj_ref, out_ref, ext_ref, acc_ref, stage_ref):
    conv_step(own_ref, near_ref, taps_ref, ext_ref, acc_ref, True)

    @pl.when(pl.program_id(0) == 8)
    def _():
        grad = acc_ref[...].astype(BF)

        def tile_of(tile):
            value = dot(grad, proj_ref[tile * 128 : (tile + 1) * 128, :], NT)
            return value[: 2 * ROWS], value[2 * ROWS :]

        write_columns(tile_of, out_ref, stage_ref, 0)


def project_body(in_ref, proj_ref, first_ref, second_ref, att_ref, stage_ref):
    for tile in range(8):
        for frame, cols in frame_rows(heads_of(in_ref, tile, 0), tile, stage_ref):
            for col in range(2):
                row = (col * 2 + frame) * ROWS
                att_ref[row : row + ROWS, tile * 128 : (tile + 1) * 128] = cols[col].astype(BF)
    out = dot(att_ref[...], proj_ref[...]).astype(BF)
    first_ref[...] = out[: 2 * ROWS].reshape(first_ref.shape)
    second_ref[...] = out[2 * ROWS :].reshape(second_ref.shape)


def unpack_body(in_ref, gq_ref, gk_ref, gv_ref, stage_ref):
    for tile in range(8):
        store_tokens(heads_of(in_ref, tile, 0), tile, gq_ref, stage_ref.at[0])
        first = heads_of(in_ref, tile, 1)
        second = heads_of(in_ref, tile, 2)
        store_tokens((first[0], second[0]), tile, gk_ref, stage_ref.at[1])
        store_tokens((first[1], second[1]), tile, gv_ref, stage_ref.at[2])


def join_columns(value, out_ref, base, roll_low):
    lane = lax.broadcasted_iota(jnp.int32, (1, 128), 1)
    for x in range(4):
        first = value[x * 128 : x * 128 + 64]
        second = value[x * 128 + 64 : (x + 1) * 128]
        if roll_low:
            first = pltpu.roll(first, HEAD, 1)
        else:
            second = pltpu.roll(second, HEAD, 1)
        out_ref[pl.ds(pl.multiple_of(base + x * 64, 64), 64), :] = jnp.where(
            lane < HEAD, first, second
        ).astype(BF)


def split_columns(value, out_ref, group, high):
    lane = lax.broadcasted_iota(jnp.int32, (1, 128), 1)
    keep = lane >= HEAD if high else lane < HEAD
    moved = pltpu.roll(value, HEAD, 1)
    first, second = (moved, value) if high else (value, moved)
    out_ref[group * 128 : group * 128 + 64, :] = jnp.where(keep, first, 0.0).astype(BF)
    out_ref[group * 128 + 64 : (group + 1) * 128, :] = jnp.where(keep, second, 0.0).astype(BF)


def forward_body(number, first, last, *refs):
    refs = list(refs)
    kv_refs = [refs.pop(0) for _ in range(number)]
    source_ref = refs.pop(0)
    if not first:
        seed_ref = refs.pop(0)
    if last:
        do_ref = refs.pop(0)
        att_ref, stat_ref, grad_ref, kv_ref, max_ref, acc_ref, sems = refs
        query_ref = source_ref
    elif first:
        query_ref, state_ref, kv_ref, max_ref, acc_ref, sems = refs
    else:
        state_ref, kv_ref, max_ref, acc_ref, sems = refs
        query_ref = source_ref
    lane = lax.broadcasted_iota(jnp.int32, (1, 128), 1)
    one = jnp.ones((), BF)
    copies = [
        pltpu.make_async_copy(kv_refs[i], kv_ref.at[:, :, i], sems.at[i]) for i in range(number)
    ]
    for copy in copies:
        copy.start()
    for group in range(16):
        rows = slice(group * 8, (group + 1) * 8)
        if first:
            value = source_ref[rows].astype(F32).reshape(64, 128) * HEAD**-0.5
            split_columns(value, query_ref, group, False)
        if last:
            split_columns(do_ref[rows].astype(F32).reshape(64, 128), grad_ref, group, True)
    for copy in copies:
        copy.wait()

    def per_block(block, _):
        start = block * TOK
        rows = pl.ds(pl.multiple_of(start, TOK), TOK)
        if first:
            max_ref[...] = jnp.full(max_ref.shape, NEGATIVE, F32)
            acc_ref[...] = jnp.zeros(acc_ref.shape, F32)
        else:
            max_ref[...] = jnp.broadcast_to(seed_ref[rows, 1:2], max_ref.shape)
            acc_ref[...] = seed_ref[rows, :]

        def update(part, scores, keys):
            before = max_ref[part, :]
            high = jnp.max(scores, axis=1, keepdims=True)
            after = jnp.maximum(before, jnp.broadcast_to(high, before.shape))
            shift = jnp.concatenate([after] * (scores.shape[1] // 128), axis=1)
            weights = jnp.exp(scores - shift).astype(BF)
            moved = dot(weights, jnp.where(lane < HEAD, one, keys))
            acc_ref[part, :] = acc_ref[part, :] * jnp.exp(before - after) + moved
            max_ref[part, :] = after

        def whole(index, _):
            keys = kv_ref[index].reshape(number * TOK, 128)
            update(slice(None), dot(query_ref[rows, :], keys, NT), keys)
            return 0

        lax.fori_loop(0, block, whole, 0)
        width = 128 if number == 2 else 256
        for part in range(TOK // width):
            count = TOK - width * part
            query = query_ref[pl.ds(pl.multiple_of(start + part * width, width), count), :]
            each = width // 128
            keys = kv_ref[block, each * part : each * (part + 1)].reshape(number * width, 128)
            row = lax.broadcasted_iota(jnp.int32, (count, 1), 0)
            key = lax.broadcasted_iota(jnp.int32, (1, number * width), 1)
            hidden = row // 128 * 2 + row % 2 < key // (number * 128) * 2 + key % 2
            scores = jnp.where(hidden, NEGATIVE, dot(query, keys, NT))
            update(slice(part * width, TOK), scores, keys)
        acc = acc_ref[...]
        if not last:
            state_ref[rows, :] = jnp.where(lane == 1, max_ref[...], acc)
            return 0
        total = acc[:, 0:1]
        att = (acc / total).astype(BF).astype(F32)
        delta = jnp.sum(att * grad_ref[rows, :].astype(F32), axis=1, keepdims=True)
        logsum = max_ref[:, 0:1] + jnp.log(total)
        stat_ref[:, rows] = jnp.where(lane == 0, logsum, delta).T[0:8, :]
        join_columns(att, att_ref, block * 256, True)
        return 0

    lax.fori_loop(0, 4, per_block, 0)


def backward_body(first, last, same_ref, other_ref, query_ref, grad_ref, stat_ref, *refs):
    refs = list(refs)
    seed_ref = None if first else refs.pop(0)
    same_out, other_out, dq_out, kv_ref, turned_ref, acc_ref, dq_ref = refs
    eye = (
        lax.broadcasted_iota(jnp.int32, (128, 128), 0)
        == lax.broadcasted_iota(jnp.int32, (128, 128), 1)
    ).astype(BF)
    kv_ref[:, :, 0] = same_ref[...]
    kv_ref[:, :, 1] = other_ref[...]
    dq_ref[...] = jnp.zeros(dq_ref.shape, F32) if first else seed_ref[...]

    def per_keys(block, _):
        turned_ref[...] = dot(eye, kv_ref[block].reshape(2 * TOK, 128), NT).astype(BF)
        acc_ref[...] = jnp.zeros(acc_ref.shape, F32)

        def pairs(start, count, part, masked):
            rows = pl.ds(pl.multiple_of(start, 128), count)
            query = query_ref[rows, :]
            grad = grad_ref[rows, :]
            stats = stat_ref[:, rows]
            keys = kv_ref[block].reshape(2 * TOK, 128)[part]
            probs = jnp.exp(dot(keys, query, NT) - stats[0:1, :])
            if masked:
                key = lax.broadcasted_iota(jnp.int32, (keys.shape[0], 1), 0)
                row = lax.broadcasted_iota(jnp.int32, (1, count), 1)
                hidden = key // 256 * 2 + key % 2 > row // 128 * 2 + row % 2
                probs = jnp.where(hidden, 0.0, probs)
            inner = (probs * (dot(keys, grad, NT) - stats[1:2, :])).astype(BF)
            acc_ref[part, :] += dot(inner, query) + dot(probs.astype(BF), grad)
            dq_ref[:, rows] += dot(turned_ref[:, part], inner)

        def whole(later, _):
            pairs(later * TOK, TOK, slice(0, 2 * TOK), False)
            return 0

        lax.fori_loop(block + 1, 4, whole, 0)
        pairs(block * TOK, TOK, slice(0, TOK), True)
        pairs(block * TOK + 256, 256, slice(TOK, 2 * TOK), True)
        total = acc_ref[...].astype(BF).reshape(4, 2, 128, 128)
        same_out[block] = total[:, 0]
        other_out[block] = total[:, 1]
        return 0

    lax.fori_loop(0, 4, per_keys, 0)
    if last:
        for block in range(4):
            value = (dq_ref[:, block * TOK : (block + 1) * TOK] * HEAD**-0.5).T
            join_columns(value, dq_out, block * 256, False)
    else:
        dq_out[...] = dq_ref[...]


def shift_y(value, steps):
    return lax.ppermute(value, "y", [(i, (i + steps) % 4) for i in range(4)])


def swap_core(value):
    return lax.ppermute(value, "c", [(0, 1), (1, 0)])


def halo(cols, forward):
    step = 1 if forward else -1

    def turn(value, cols):
        pairs = [(i, (i + cols) % 8) for i in range(8)]
        return lax.ppermute(value, ("z", "c"), pairs)

    left = turn(cols[1], 1)
    right = turn(cols[0], -1)
    wide = jnp.stack([left, *cols, right])
    frames = [(t, t + step) for t in range(16) if 0 <= t + step < 16]
    return wide, lax.ppermute(wide, ("y", "x"), frames)


def exchange_all(value):
    split = value.reshape(128, -1, 128)
    return lax.all_to_all(split, AXES, split_axis=0, concat_axis=0, tiled=True)


def columns_first(array):
    return array.transpose(2, 0, 1, 3)


def flat(array):
    return array.reshape(2 * ROWS, 2, -1)


def tokens_back(array):
    return array.reshape(2, 2, ROWS, -1).transpose(1, 2, 0, 3)


def shards(queries, key_rows, value_rows, out_proj, conv_taps, cotangent):
    channels = out_proj.shape[1]
    stage = pltpu.VMEM((16, 2 * ROWS + 8, 128), F32)
    taps_spec = pl.BlockSpec((1, 1, 3, channels, channels), lambda t: (t // 3, t % 3, 0, 0, 0))
    conv_scratch = [
        pltpu.VMEM((3, 4, 4, ROWS, channels), BF),
        pltpu.VMEM((4 * ROWS, channels), F32),
    ]
    grouped = (4, 4, 128, 128)

    near = halo(tuple(columns_first(cotangent)), False)
    (packed,) = kernel_call(
        pack_body,
        [struct((4, 16, 2, 3, 8, 128))],
        [stage],
        (flat(queries), flat(key_rows), flat(value_rows)),
        us=4.0,
    )
    packed = exchange_all(packed)
    (grad,) = kernel_call(
        adjoint_body,
        [struct((4, 16, 2, 1, 8, 128))],
        [*conv_scratch, stage],
        (*near, conv_taps, out_proj),
        grid=(9,),
        specs={2: taps_spec},
        us=12.0,
    )
    packed, grad = lax.optimization_barrier((packed, grad))
    kv_same = {0: packed[:, 8:].reshape(grouped)}
    for steps in (1, 3, 2):
        kv_same[steps] = shift_y(kv_same[0], steps)
    kv_other = {steps: swap_core(kv_same[steps]) for steps in (0, 1, 3, 2)}
    grad = exchange_all(grad)

    def attend(arrays, extra, outs, us, first=False, last=False):
        number = len(arrays)
        specs = {index: pl.BlockSpec(memory_space=pl.ANY) for index in range(number)}
        if first:
            specs[number] = pl.BlockSpec((128, 8, 128), lambda *_: (0, 0, 0))
        return kernel_call(
            functools.partial(forward_body, number, first, last),
            outs,
            [
                pltpu.VMEM((4, 4, number, 128, 128), BF),
                pltpu.VMEM((TOK, 128), F32),
                pltpu.VMEM((TOK, 128), F32),
                pltpu.SemaphoreType.DMA((number,)),
            ],
            (*arrays, *extra),
            specs=specs,
            us=us,
        )

    state = struct((SPAN, 128), F32)
    query, seed = attend(
        [kv_same[0], kv_other[0]], (packed,), [struct((SPAN, 128)), state], 10.0, True
    )
    rest = [kv_same[i] for i in (1, 3, 2)] + [kv_other[i] for i in (1, 3, 2)]
    att, stats, grad = attend(
        rest,
        (query, seed, grad),
        [struct((SPAN // 2, 128)), struct((8, SPAN), F32), struct((SPAN, 128))],
        25.0,
        last=True,
    )
    att = exchange_all(att).reshape(4, 16, 2, 1, 8, 128)

    seed = None
    total = None
    for steps in (2, 1, 3, 0):
        last = steps == 0
        same, other, seed = kernel_call(
            functools.partial(backward_body, seed is None, last),
            [
                struct(grouped),
                struct(grouped),
                struct((SPAN // 2, 128)) if last else struct((128, SPAN), F32),
            ],
            [
                pltpu.VMEM((4, 4, 2, 128, 128), BF),
                pltpu.VMEM((128, 2 * TOK), BF),
                pltpu.VMEM((2 * TOK, 128), F32),
                pltpu.VMEM((128, SPAN), F32),
            ],
            (kv_same[steps], kv_other[steps], query, grad, stats)
            + (() if seed is None else (seed,)),
            us=16.0,
        )
        joined = same.astype(F32) + swap_core(other).astype(F32)
        if not last:
            joined = shift_y(joined.astype(BF), 4 - steps).astype(F32)
        total = joined if total is None else total + joined
    projected = kernel_call(
        project_body,
        [struct((2, ROWS, channels))] * 2,
        [pltpu.VMEM((4 * ROWS, 1024), BF), stage],
        (att, out_proj),
        us=3.0,
    )
    near = halo(projected, True)
    (conv,) = kernel_call(
        conv_body,
        [struct((4 * ROWS, channels))],
        conv_scratch,
        (*near, conv_taps),
        grid=(9,),
        specs={2: taps_spec},
        us=10.0,
    )
    grads = jnp.concatenate(
        [seed.reshape(128, 8, 128), total.astype(BF).reshape(128, 16, 128)], axis=1
    )
    grads = exchange_all(grads).reshape(4, 16, 2, 3, 8, 128)
    grads = kernel_call(
        unpack_body,
        [struct((2 * ROWS, 2, 1024))] * 3,
        [pltpu.VMEM((3, 16, 2 * ROWS + 8, 128), F32)],
        (grads,),
        us=4.0,
    )
    return (tokens_back(conv), *(g.reshape(queries.shape) for g in grads))


def solution(mesh):
    grid = Mesh(mesh.devices.reshape(4, 4, 4, 2), AXES)
    spec = P(("y", "x"), None, ("z", "c"), None)
    return jax.shard_map(
        shards,
        mesh=grid,
        in_specs=(spec, spec, spec, P(), P(), spec),
        out_specs=(spec,) * 4,
        check_vma=False,
    )
```
